1024 devices in a mesh: dp: 8 (over y), mp: 128 (over x, z, core).
Axes of the slice: x: 4, y: 8, z: 16, core: 2. Of those that a mesh axis runs over, the one named last changes fastest.
Arguments:
- inputs: bfloat16 [1024, 2560], P('dp'), may hold values from -6 to 6
- cotangent: bfloat16 [1024, 2560], P('dp'), may hold values from -6 to 6
- w_in: bfloat16 [128, 16, 128, 128], P('mp', 'dp'), may hold values from -0.125 to 0.125
- w_out: bfloat16 [128, 16, 128, 128], P('mp', 'dp'), may hold values from -0.0546875 to 0.0546875
- block_index: int32 [128, 16], P('mp'), may hold values from 0 to 19, as said below
- block_count: int32 [128], P('mp'), may hold values from 8 to 16, as said below
- drop_seeds: int32 [1024], P('dp'), may hold values from 0 to 1073741823
Outputs:
- outputs: bfloat16 [1024, 2560], P(('dp', 'mp'))
- input_grad: bfloat16 [1024, 2560], P(('dp', 'mp'))
- w_in_grad: float32 [128, 16, 128, 128], P('mp', 'dp')
- w_out_grad: float32 [128, 16, 128, 128], P('mp', 'dp')
The draws below stay inside these ranges and needn't reach their ends.
Inputs may be any that keep to these rules, and one draw needn't show every extreme that they name: `block_index`: each row holds 16 different feature blocks; the first slots hold a few shared blocks and the blocks of a butterfly over the feature blocks. `block_count`: some hidden block uses all 16 slots and some uses 16 // 2.
All inputs are finite; a program needn't handle non-finite values.
Results may differ from the reference program's by a relative error of at most 0.012.
Values may be sent and summed in bfloat16 or wider, within the bound.
A program may use at most 32 MiB of HBM per device.

```python
import math
import jax
import jax.numpy as jnp
from jax import lax

D = 2560
BS = 128
K = 16
HBLOCKS = 128
TOK_G = 128
TOKENS = 1024
N_DP = 8


def draw_block_index(key, part):
    block_cols = D // BS
    glob_count = max(1, block_cols // 10)
    fly_width = 2 ** int(math.floor(math.log2(block_cols - glob_count)))
    fly_levels = fly_width.bit_length() - 1
    column_order = jax.random.permutation(jax.random.fold_in(key, 1), block_cols).astype(jnp.int32)
    row_ids = jnp.arange(HBLOCKS, dtype=jnp.int32)
    fly_base = row_ids % fly_width
    column_ids = jnp.arange(block_cols, dtype=jnp.int32)
    priority = jnp.zeros((HBLOCKS, block_cols), jnp.int32)
    for glob_slot in range(glob_count):
        priority = priority | (column_ids[None, :] == column_order[glob_slot]).astype(jnp.int32)
    fly_cols = column_order[glob_count:glob_count + fly_width]
    priority = priority | (column_ids[None, :] == fly_cols[fly_base][:, None]).astype(jnp.int32)
    for fly_level in range(fly_levels):
        partner = fly_cols[fly_base ^ 1 << fly_level]
        priority = priority | (column_ids[None, :] == partner[:, None]).astype(jnp.int32)
    random_part = jax.random.randint(jax.random.fold_in(key, 2), (HBLOCKS, block_cols), 0, 1 << 20) * 64 + column_ids[None, :]
    sort_key = random_part - priority * (1 << 27)
    return jnp.argsort(sort_key, axis=1, stable=True)[:, :K].astype(jnp.int32)


def draw_block_count(key, part):
    counts = jax.random.randint(jax.random.fold_in(key, 3), (HBLOCKS,), K // 2, K + 1).astype(jnp.int32)
    first_pos = jax.random.randint(jax.random.fold_in(key, 4), (), 0, HBLOCKS)
    second_pos = (first_pos + 1 + jax.random.randint(jax.random.fold_in(key, 5), (), 0, HBLOCKS - 1)) % HBLOCKS
    return counts.at[first_pos].set(K).at[second_pos].set(K // 2).astype(jnp.int32)


def with_ends(values, own_key, least, high):
    longest = values.shape.index(max(values.shape))
    spots = []
    for shift in (0, 1):
        where = [jax.random.randint(jax.random.fold_in(own_key, axis), (), 0, length) for axis, length in enumerate(values.shape)]
        where[longest] = (where[longest] + shift) % values.shape[longest]
        spots.append(tuple(where))
    return values.at[spots[0]].set(least).at[spots[1]].set(high)


def levels(key, dims, shards, smallest, top_value):
    def one(dim, parts):
        steps = jax.random.uniform(jax.random.fold_in(jax.random.fold_in(key, 6), dim), (parts,), jnp.float32, smallest / len(shards), top_value / len(shards))
        return jnp.repeat(jnp.exp(steps), dims[dim] // parts).reshape((-1,) + (1,) * (len(dims) - dim - 1))

    level = one(*shards[0])
    for cut in shards[1:]:
        level = level * one(*cut)
    return level


def scatter_about(rng, extent, deviation, most, shards=(), held_as=jnp.bfloat16):
    values = jax.random.normal(rng, extent, jnp.float32) * deviation
    if len(shards) > 0:
        values = levels(rng, extent, shards, -0.22, 0.18) * values
    return jnp.clip(values, min=-most, max=most).astype(held_as)


def setup_inputs(seed: int = 0) -> dict:
    keys = jax.random.split(jax.random.key(seed), 8)
    return {
        "inputs": scatter_about(keys[0], (TOKENS, D), 1.0, 6.0, ((0, 8),)),
        "cotangent": scatter_about(keys[1], (TOKENS, D), 1.0, 6.0, ((0, 8),)),
        "w_in": scatter_about(keys[2], (HBLOCKS, K, BS, BS), (BS * K) ** -0.5, 0.125, ((0, 128), (1, 8))),
        "w_out": scatter_about(keys[3], (HBLOCKS, K, BS, BS), (BS * K * HBLOCKS // (D // BS)) ** -0.5, 0.0546875, ((0, 128), (1, 8))),
        "block_index": draw_block_index(jax.random.fold_in(keys[7], 71), 0),
        "block_count": draw_block_count(jax.random.fold_in(keys[7], 71), 0),
        "drop_seeds": with_ends(jax.random.randint(keys[6], (TOKENS,), 0, 1073741824), jax.random.fold_in(keys[6], 1), 0, 1073741823).astype(jnp.int32),
    }


def scramble(value):
    value = value ^ lax.shift_right_logical(value, jnp.int32(16))
    value = value * jnp.int32(73244475)
    value = value ^ lax.shift_right_logical(value, jnp.int32(16))
    value = value * jnp.int32(73244475)
    value = value ^ lax.shift_right_logical(value, jnp.int32(16))
    return value

def keep_factor(seeds, first_unit):
    units = first_unit + jnp.arange(BS, dtype=jnp.int32)
    mixed = scramble(seeds[:, None] + units[None, :] * jnp.int32(668265261))
    kept = mixed & jnp.int32(7) != jnp.int32(0)
    return kept.astype(jnp.float32) * jnp.float32(8.0 / 7.0)

def gelu_parts(pre_act):
    coeff = math.sqrt(2.0 / math.pi)
    inner = coeff * (pre_act + 0.044715 * pre_act ** 3)
    tanh_val = jnp.tanh(inner)
    activation = 0.5 * pre_act * (1.0 + tanh_val)
    slope = 0.5 * (1.0 + tanh_val) + 0.5 * pre_act * (1.0 - tanh_val * tanh_val) * coeff * (1.0 + 3.0 * 0.044715 * pre_act * pre_act)
    return (activation, slope)

def round_half(value):
    return lax.optimization_barrier(value.astype(jnp.bfloat16)).astype(jnp.float32)

def reference(inputs, cotangent, w_in, w_out, block_index, block_count, drop_seeds):
    block_cols = D // BS
    tok_blocks = inputs.reshape(TOKENS, block_cols, BS)
    cot_blocks = cotangent.reshape(TOKENS, block_cols, BS)
    slot_ids = jnp.arange(K, dtype=jnp.int32)
    col_ids = jnp.arange(block_cols, dtype=jnp.int32)

    def one_block(carry, item):
        out_acc, in_acc = carry
        hidden_id, idx_row, count, w_first, w_second = item
        valid = (slot_ids < count).astype(jnp.bfloat16)
        w1m = (w_first * valid[:, None, None]).astype(jnp.float32)
        w2m = (w_second * valid[:, None, None]).astype(jnp.float32)
        selected = jnp.take(tok_blocks, idx_row, axis=1).astype(jnp.float32)
        cot_sel = jnp.take(cot_blocks, idx_row, axis=1).astype(jnp.float32)
        pre_act = jnp.einsum('tkc,kcf->tf', selected, w1m)
        activation, slope = gelu_parts(pre_act)
        keep_scale = keep_factor(drop_seeds, hidden_id * BS)
        dropped = (activation * keep_scale).astype(jnp.bfloat16)
        one_hot = (idx_row[:, None] == col_ids[None, :]).astype(jnp.float32)
        out_blocks = jnp.einsum('tf,kfc->tkc', dropped.astype(jnp.float32), w2m)
        out_term = jnp.einsum('tkc,kd->tdc', out_blocks, one_hot).reshape(TOKENS, D)
        out_acc = out_acc + out_term
        grad_drop = jnp.einsum('tkc,kfc->tf', cot_sel, w2m)
        grad_pre = (grad_drop * keep_scale * slope).astype(jnp.bfloat16)
        in_blocks = jnp.einsum('tf,kcf->tkc', grad_pre.astype(jnp.float32), w1m)
        in_term = jnp.einsum('tkc,kd->tdc', in_blocks, one_hot).reshape(TOKENS, D)
        in_acc = in_acc + in_term
        valid_full = valid.astype(jnp.float32)
        group_sel = selected.reshape(N_DP, TOK_G, K, BS)
        group_cot = cot_sel.reshape(N_DP, TOK_G, K, BS)
        group_pre = grad_pre.astype(jnp.float32).reshape(N_DP, TOK_G, BS)
        group_drop = dropped.astype(jnp.float32).reshape(N_DP, TOK_G, BS)
        term_in = jnp.einsum('gtkc,gtf->gkcf', group_sel, group_pre) * valid_full[None, :, None, None]
        term_out = jnp.einsum('gtf,gtkc->gkfc', group_drop, group_cot) * valid_full[None, :, None, None]
        term_in = round_half(term_in)
        term_out = round_half(term_out)
        return ((out_acc, in_acc), (lax.optimization_barrier(jnp.sum(term_in, axis=0)), lax.optimization_barrier(jnp.sum(term_out, axis=0))))
    start = (jnp.zeros((TOKENS, D), jnp.float32), jnp.zeros((TOKENS, D), jnp.float32))
    hidden_ids = jnp.arange(HBLOCKS, dtype=jnp.int32)
    (out_acc, in_acc), (grad_in, grad_out) = lax.scan(one_block, start, (hidden_ids, block_index, block_count, w_in, w_out))
    return (out_acc.astype(jnp.bfloat16), in_acc.astype(jnp.bfloat16), grad_in, grad_out)
```

```python
import math

import jax
import jax.numpy as jnp
from jax import lax
from jax.experimental import pallas as pl
from jax.experimental.pallas import tpu as pltpu
from jax.sharding import PartitionSpec as P

BS = 128
K = 16
NJ = 20
HJ = NJ // 2
NY = 8
NX = 4
NZ = 16
MESH = pl.DeviceIdType.MESH
F32 = jnp.float32
BF16 = jnp.bfloat16
Z_ORDER = (8, 7, 9, 6, 10, 5, 11, 4, 12, 3, 13, 2, 14, 1, 15)


def scramble(value):
    for _ in range(2):
        value = value ^ lax.shift_right_logical(value, jnp.int32(16))
        value = value * jnp.int32(73244475)
    return value ^ lax.shift_right_logical(value, jnp.int32(16))


def gelu_parts(pre_act):
    coeff = math.sqrt(2.0 / math.pi)
    square = pre_act * pre_act
    inner = coeff * (pre_act + 0.044715 * (square * pre_act))
    tanh_val = jnp.tanh(inner)
    activation = 0.5 * pre_act * (1.0 + tanh_val)
    slope = 0.5 * (1.0 + tanh_val) + 0.5 * pre_act * (1.0 - tanh_val * tanh_val) * coeff * (
        1.0 + 3.0 * 0.044715 * square
    )
    return activation, slope


def mm(a, b):
    return lax.dot_general(a, b, (((1,), (0,)), ((), ())), preferred_element_type=F32)


def mm_t(a, b):
    return lax.dot_general(a, b, (((1,), (1,)), ((), ())), preferred_element_type=F32)


def rdma(src, dst, send_sem, recv_sem, device):
    return pltpu.make_async_remote_copy(
        src_ref=src, dst_ref=dst, send_sem=send_sem, recv_sem=recv_sem,
        device_id=device, device_id_type=MESH,
    )


def ag_slots(step, way):
    return (0, 1) if step < NY // 2 else (way,)


def rs_slots(step, way):
    return (0, 1) if step > 1 else (way,)


def kernel(
    x_hbm, g_hbm, wi_hbm, wo_hbm, idx_ref, cnt_ref, seed_ref,
    out_ref, ing_ref, gwi_ref, gwo_ref,
    x3, g3, x3t, wg, keep_ref, perm_ref, pre_ref, gd_ref, dt_ref, gp_ref,
    rs_send, rs_recv, c_send, c_recv, own, x_send, x_recv, zsum, z_send, z_recv,
    idxv, inv,
    ld_sem, wl_sem, ag_ss, ag_rs, rs_ss, rs_rs, c_ss, c_rs, x_ss, x_rs, z_ss, z_rs, ready,
):
    y = lax.axis_index("dp")
    mp = lax.axis_index("mp")
    core = lax.rem(mp, 2)
    z = lax.rem(lax.div(mp, 2), NZ)
    x = lax.div(mp, 2 * NZ)

    def at(yy, xx, zz, cc):
        return (yy, (xx * NZ + zz) * 2 + cc)

    def wrap(value, size):
        return lax.rem(value + size, size)

    y_dev = (at(wrap(y + 1, NY), x, z, core), at(wrap(y - 1, NY), x, z, core))
    x_dev = (at(y, wrap(x + 1, NX), z, core), at(y, wrap(x - 1, NX), z, core))
    pair_dev = at(y, x, z, 1 - core)

    def z_dev(shift):
        return at(y, x, wrap(z + shift, NZ), core)

    w_hbm = (wi_hbm, wo_hbm)

    loads = []
    for j in range(NJ):
        cols = pl.ds(j * BS, BS)
        loads.append(pltpu.make_async_copy(x_hbm.at[:, cols], x3.at[j], ld_sem.at[0, j]))
        loads.append(pltpu.make_async_copy(g_hbm.at[:, cols], g3.at[j], ld_sem.at[1, j]))
    own_w = [
        pltpu.make_async_copy(w_hbm[w].at[0], wg.at[w, pl.ds(2 * y, 2)], wl_sem.at[w])
        for w in range(2)
    ]

    barrier = pltpu.get_barrier_semaphore()
    around = (*y_dev, *x_dev, z_dev(1), z_dev(-1), pair_dev)
    for device in around:
        pl.semaphore_signal(barrier, inc=1, device_id=device, device_id_type=MESH)
    for copy in own_w + loads:
        copy.start()
    pl.semaphore_wait(barrier, len(around))

    def ag_origin(step, way):
        return wrap(y - step if way == 0 else y + step, NY)

    def ag_copy(w, step, way, s):
        slot = 2 * ag_origin(step - 1, way) + s
        src = w_hbm[w].at[0, s] if step == 1 else wg.at[w, slot]
        return rdma(
            src, wg.at[w, slot], ag_ss.at[w, way, step - 1, s], ag_rs.at[w, way, step - 1, s],
            y_dev[way],
        )

    def ag_wait(w, step, way, s):
        here = wg.at[w, 2 * ag_origin(step, way) + s]
        rdma(
            here, here, ag_ss.at[w, way, step - 1, s], ag_rs.at[w, way, step - 1, s], y_dev[way]
        ).wait_recv()

    sends = []

    def start(copy):
        copy.start()
        sends.append(copy)

    for w in range(2):
        for s in range(2):
            for way in range(2):
                start(ag_copy(w, 1, way, s))

    for k in range(K):
        idxv[k] = jnp.where(k < cnt_ref[0], idx_ref[0, k], NJ)
    for j in range(NJ):
        found = jnp.int32(K)
        for k in range(K):
            found = jnp.where(idxv[k] == j, k, found)
        inv[j] = found
    blank = jnp.zeros((BS, BS), BF16)
    x3[NJ] = blank
    g3[NJ] = blank
    wg[0, K] = blank
    wg[1, K] = blank

    rows = lax.broadcasted_iota(jnp.int32, (BS, BS), 0)
    cols = lax.broadcasted_iota(jnp.int32, (BS, BS), 1)
    seeds = jnp.broadcast_to(seed_ref[...], (BS, BS)).T
    mixed = scramble(seeds + (mp * BS + cols) * jnp.int32(668265261))
    keep_ref[...] = jnp.where((mixed & 7) != 0, F32(8.0 / 7.0), F32(0.0))
    half = lax.shift_right_logical(rows, 6)
    tok_x = (x + (lax.shift_right_logical(rows, 4) & 3)) & 3
    tok_z = (z + (rows & 15)) & 15
    tok_c = jnp.where(half == 1, core, 1 - core)
    token = tok_x * 32 + tok_z * 2 + tok_c
    perm_ref[...] = jnp.where(token == cols, F32(1.0), F32(0.0)).astype(BF16)

    for copy in loads:
        copy.wait()

    def ready_round(r):
        for shift in (1 << r, -(1 << r)):
            pl.semaphore_signal(
                ready.at[r], inc=1, device_id=z_dev(shift), device_id_type=MESH
            )

    ready_round(0)
    for k in range(K):
        x3t[k] = x3[idxv[k]].T

    def two(ref, origin):
        return ref[idxv[2 * origin]], ref[idxv[2 * origin + 1]]

    def pre_part(origin):
        left = jnp.concatenate(two(x3, origin), axis=1)
        right = wg[0, pl.ds(2 * origin, 2)].reshape(2 * BS, BS)
        return mm(left, right)

    def gd_part(origin):
        left = jnp.concatenate(two(g3, origin), axis=1)
        right = jnp.concatenate((wg[1, 2 * origin], wg[1, 2 * origin + 1]), axis=1)
        return mm_t(left, right)

    for copy in own_w:
        copy.wait()
    pre_ref[...] = pre_part(y)
    gd_ref[...] = gd_part(y)

    def ag_step(w, step):
        for s in range(2):
            for way in range(2):
                if s in ag_slots(step, way):
                    ag_wait(w, step, way, s)
                    if step < NY // 2 and s in ag_slots(step + 1, way):
                        start(ag_copy(w, step + 1, way, s))
        acc, part = ((pre_ref, pre_part), (gd_ref, gd_part))[w]
        if step < NY // 2:
            acc[...] += part(ag_origin(step, 0)) + part(ag_origin(step, 1))
        else:
            acc[...] += part(ag_origin(step, 0))

    for step in range(1, NY // 2 + 1):
        ag_step(0, step)
        if step <= 3:
            pl.semaphore_wait(ready.at[step - 1], 2)
            if step < 3:
                ready_round(step)
        ag_step(1, step)

    keep = keep_ref[...]
    activation, slope = gelu_parts(pre_ref[...])
    dropped = (activation * keep).astype(BF16)
    grad_pre = (gd_ref[...] * keep * slope).astype(BF16)
    gp_ref[...] = grad_pre
    dt_ref[...] = dropped.T
    perm = perm_ref[...]
    ordered = (mm(perm, dropped).astype(BF16), mm(perm, grad_pre).astype(BF16))

    def placed(t, j, lo):
        part = ordered[t][lo:lo + 64]
        if t == 0:
            return mm(part, jnp.concatenate((wg[1, inv[j]], wg[1, inv[j + 1]]), axis=1))
        return mm_t(part, jnp.concatenate((wg[0, inv[j]], wg[0, inv[j + 1]]), axis=0))

    def c_copy(t, h):
        return rdma(c_send.at[t, h], c_recv.at[t, h], c_ss.at[t, h], c_rs.at[t, h], pair_dev)

    for t in range(2):
        for h in range(2):
            for j in range(0, HJ, 2):
                both = placed(t, h * HJ + j, 0).astype(BF16)
                c_send[t, h, j] = both[:, :BS]
                c_send[t, h, j + 1] = both[:, BS:]
            start(c_copy(t, h))

    def term(w, slot):
        if w == 1:
            return mm(dt_ref[...], g3[idxv[slot]])
        return mm(x3t[slot], gp_ref[...])

    def rs_copy(w, step, way, s):
        return rdma(
            rs_send.at[w, way, step - 1, s], rs_recv.at[w, way, step - 1, s],
            rs_ss.at[w, way, step - 1, s], rs_rs.at[w, way, step - 1, s], y_dev[way],
        )

    def rs_piece(w, step, way, s):
        far = NY // 2 + 1 - step
        owner = wrap(y + far if way == 0 else y - far, NY)
        value = term(w, 2 * owner + s)
        if step > 1 and s in rs_slots(step - 1, way):
            rs_copy(w, step - 1, way, s).wait_recv()
            value = value + rs_recv[w, way, step - 2, s].astype(F32)
        rs_send[w, way, step - 1, s] = value.astype(BF16)
        start(rs_copy(w, step, way, s))

    def rs_step(step):
        for w in (1, 0):
            for s in range(2):
                for way in range(2):
                    if s in rs_slots(step, way):
                        rs_piece(w, step, way, s)

    rs_step(1)
    for t in range(2):
        for h in range(2):
            for j in range(0, HJ, 2):
                both = placed(t, h * HJ + j, 64)
                own[t, h, j] = both[:, :BS]
                own[t, h, j + 1] = both[:, BS:]

    X_WAY = (0, 1, 0, 1, 0, 1)
    X_HALF = (0, 1, 1, 0, 0, 1)
    X_CHUNK = (2, 2, 1, 3, 1, 3)

    def x_copy(t, p):
        return rdma(x_send.at[t, p], x_recv.at[t, p], x_ss.at[t, p], x_rs.at[t, p], x_dev[X_WAY[p]])

    def x_own(t, h, chunk):
        span = pl.ds(chunk * 16, 16)
        return own[t, h, :, span, :] + c_recv[t, h, :, span, :].astype(F32)

    for t in range(2):
        for h in range(2):
            c_copy(t, h).wait_recv()
        for p in range(4):
            x_send[t, p] = x_own(t, X_HALF[p], X_CHUNK[p]).astype(BF16)
            start(x_copy(t, p))

    rs_step(2)

    for t in range(2):
        for p in (4, 5):
            x_copy(t, p - 4).wait_recv()
            value = x_own(t, X_HALF[p], X_CHUNK[p]) + x_recv[t, p - 4].astype(F32)
            x_send[t, p] = value.astype(BF16)
            start(x_copy(t, p))

    rs_step(3)

    def z_copy(t, shift):
        return rdma(
            z_send.at[t, shift], z_recv.at[t, shift], z_ss.at[t, shift], z_rs.at[t, shift],
            z_dev(shift),
        )

    for t in range(2):
        for h, (near, far) in enumerate(((3, 4), (2, 5))):
            x_copy(t, near).wait_recv()
            x_copy(t, far).wait_recv()
            value = (
                x_own(t, h, 0) + x_recv[t, near].astype(F32) + x_recv[t, far].astype(F32)
            )
            zsum[t, pl.ds(h * HJ * 16, HJ * 16)] = value.reshape(HJ * 16, BS)
        for shift in Z_ORDER:
            z_send[t, shift] = zsum[t, pl.ds(shift, NJ, stride=16), :].astype(BF16)
            start(z_copy(t, shift))

    rs_step(4)

    for t, o_ref in enumerate((out_ref, ing_ref)):
        total = zsum[t, pl.ds(0, NJ, stride=16), :]
        for shift in Z_ORDER:
            z_copy(t, shift).wait_recv()
            total = total + z_recv[t, shift].astype(F32)
        o_ref[...] = total.astype(BF16)

    for w, o_ref in ((1, gwo_ref), (0, gwi_ref)):
        for s in range(2):
            value = term(w, 2 * y + s)
            for way in range(2):
                rs_copy(w, NY // 2, way, s).wait_recv()
                value = value + rs_recv[w, way, NY // 2 - 1, s].astype(F32)
            o_ref[0, s] = value

    for copy in sends:
        copy.wait_send()


def body(inputs, cotangent, w_in, w_out, block_index, block_count, drop_seeds):
    vmem = pl.BlockSpec(memory_space=pltpu.VMEM)
    smem = pl.BlockSpec(memory_space=pltpu.SMEM)
    anywhere = pl.BlockSpec(memory_space=pl.ANY)
    dma = pltpu.SemaphoreType.DMA
    block = (BS, BS)
    out, ing, gwi, gwo = pl.pallas_call(
        kernel,
        out_shape=(
            jax.ShapeDtypeStruct((NJ, BS), BF16),
            jax.ShapeDtypeStruct((NJ, BS), BF16),
            jax.ShapeDtypeStruct((1, 2, BS, BS), F32),
            jax.ShapeDtypeStruct((1, 2, BS, BS), F32),
        ),
        in_specs=[anywhere] * 4 + [smem] * 2 + [vmem],
        out_specs=(vmem,) * 4,
        scratch_shapes=[
            pltpu.VMEM((NJ + 1, *block), BF16),
            pltpu.VMEM((NJ + 1, *block), BF16),
            pltpu.VMEM((K, *block), BF16),
            pltpu.VMEM((2, K + 1, *block), BF16),
            pltpu.VMEM(block, F32),
            pltpu.VMEM(block, BF16),
            pltpu.VMEM(block, F32),
            pltpu.VMEM(block, F32),
            pltpu.VMEM(block, BF16),
            pltpu.VMEM(block, BF16),
            pltpu.VMEM((2, 2, 4, 2, *block), BF16),
            pltpu.VMEM((2, 2, 4, 2, *block), BF16),
            pltpu.VMEM((2, 2, HJ, 64, BS), BF16),
            pltpu.VMEM((2, 2, HJ, 64, BS), BF16),
            pltpu.VMEM((2, 2, HJ, 64, BS), F32),
            pltpu.VMEM((2, 6, HJ, 16, BS), BF16),
            pltpu.VMEM((2, 6, HJ, 16, BS), BF16),
            pltpu.VMEM((2, NJ * 16, BS), F32),
            pltpu.VMEM((2, NZ, NJ, BS), BF16),
            pltpu.VMEM((2, NZ, NJ, BS), BF16),
            pltpu.SMEM((K,), jnp.int32),
            pltpu.SMEM((NJ,), jnp.int32),
            dma((2, NJ)),
            dma((2,)),
            dma((2, 2, 4, 2)),
            dma((2, 2, 4, 2)),
            dma((2, 2, 4, 2)),
            dma((2, 2, 4, 2)),
            dma((2, 2)),
            dma((2, 2)),
            dma((2, 6)),
            dma((2, 6)),
            dma((2, NZ)),
            dma((2, NZ)),
            pltpu.SemaphoreType.REGULAR((3,)),
        ],
        compiler_params=pltpu.CompilerParams(
            collective_id=0, has_side_effects=True, vmem_limit_bytes=40 << 20
        ),
    )(
        inputs, cotangent, w_in, w_out, block_index, block_count,
        drop_seeds.reshape(1, BS),
    )
    return out.reshape(1, NJ * BS), ing.reshape(1, NJ * BS), gwi, gwo


def solution(mesh):
    placed = (
        P("dp", None),
        P("dp", None),
        P("mp", "dp", None, None),
        P("mp", "dp", None, None),
        P("mp", None),
        P("mp"),
        P("dp"),
    )
    return jax.shard_map(
        body,
        mesh=mesh,
        in_specs=placed,
        out_specs=(
            P(("dp", "mp"), None),
            P(("dp", "mp"), None),
            P("mp", "dp", None, None),
            P("mp", "dp", None, None),
        ),
        check_vma=False,
    )
```

```python
import contextlib
import math

import jax
import jax.numpy as jnp
from jax import lax
from jax.experimental import pallas as pl
from jax.experimental.pallas import tpu as pltpu
from jax.sharding import PartitionSpec as P

BS = 128
K = 16
NJ = 20
HJ = NJ // 2
NY = 8
NX = 4
NZ = 16
MESH = pl.DeviceIdType.MESH
F32 = jnp.float32
BF16 = jnp.bfloat16
Z_ORDER = (8, 7, 9, 6, 10, 5, 11, 4, 12, 3, 13, 2, 14, 1, 15)


def phase(name):
    return contextlib.nullcontext(name)


def scramble(value):
    for _ in range(2):
        value = value ^ lax.shift_right_logical(value, jnp.int32(16))
        value = value * jnp.int32(73244475)
    return value ^ lax.shift_right_logical(value, jnp.int32(16))


def gelu_parts(pre_act):
    coeff = math.sqrt(2.0 / math.pi)
    square = pre_act * pre_act
    inner = coeff * (pre_act + 0.044715 * (square * pre_act))
    tanh_val = jnp.tanh(inner)
    activation = 0.5 * pre_act * (1.0 + tanh_val)
    slope = 0.5 * (1.0 + tanh_val) + 0.5 * pre_act * (1.0 - tanh_val * tanh_val) * coeff * (
        1.0 + 3.0 * 0.044715 * square
    )
    return activation, slope


def mm(a, b):
    return lax.dot_general(a, b, (((1,), (0,)), ((), ())), preferred_element_type=F32)


def mm_t(a, b):
    return lax.dot_general(a, b, (((1,), (1,)), ((), ())), preferred_element_type=F32)


def rdma(src, dst, send_sem, recv_sem, device):
    return pltpu.make_async_remote_copy(
        src_ref=src, dst_ref=dst, send_sem=send_sem, recv_sem=recv_sem,
        device_id=device, device_id_type=MESH,
    )


def ag_slots(step, way):
    return (0, 1) if step < NY // 2 else (way,)


def rs_slots(step, way):
    return (0, 1) if step > 1 else (way,)


def kernel(
    x_hbm, g_hbm, wi_hbm, wo_hbm, idx_hbm, cnt_hbm, seed_hbm,
    out_ref, ing_ref, gwi_ref, gwo_ref,
    x3, g3, x3t, wg, keep_ref, perm_ref, pre_ref, gd_ref, dt_ref, gp_ref,
    rs_send, rs_recv, c_send, c_recv, own, x_send, x_recv, zsum, z_send, z_recv,
    idx_ref, cnt_ref, seed_ref, idxv, inv,
    sm_sem, ld_sem, wl_sem, ag_ss, ag_rs, rs_ss, rs_rs, c_ss, c_rs, x_ss, x_rs, z_ss, z_rs, ready,
):
    y = lax.axis_index("dp")
    mp = lax.axis_index("mp")
    core = lax.rem(mp, 2)
    z = lax.rem(lax.div(mp, 2), NZ)
    x = lax.div(mp, 2 * NZ)

    def at(yy, xx, zz, cc):
        return (yy, (xx * NZ + zz) * 2 + cc)

    def wrap(value, size):
        return lax.rem(value + size, size)

    y_dev = (at(wrap(y + 1, NY), x, z, core), at(wrap(y - 1, NY), x, z, core))
    x_dev = (at(y, wrap(x + 1, NX), z, core), at(y, wrap(x - 1, NX), z, core))
    pair_dev = at(y, x, z, 1 - core)

    def z_dev(shift):
        return at(y, x, wrap(z + shift, NZ), core)

    w_hbm = (wi_hbm, wo_hbm)

    loads = []
    for j in range(NJ):
        cols = pl.ds(j * BS, BS)
        loads.append(pltpu.make_async_copy(x_hbm.at[:, cols], x3.at[j], ld_sem.at[0, j]))
        loads.append(pltpu.make_async_copy(g_hbm.at[:, cols], g3.at[j], ld_sem.at[1, j]))
    own_w = [
        pltpu.make_async_copy(w_hbm[w].at[0], wg.at[w, pl.ds(2 * y, 2)], wl_sem.at[w])
        for w in range(2)
    ]

    barrier = pltpu.get_barrier_semaphore()
    around = (*y_dev, *x_dev, z_dev(1), z_dev(-1), pair_dev)
    for device in around:
        pl.semaphore_signal(barrier, inc=1, device_id=device, device_id_type=MESH)
    small = [
        pltpu.make_async_copy(src, dst, sm_sem.at[i])
        for i, (src, dst) in enumerate(
            ((idx_hbm, idx_ref), (seed_hbm, seed_ref))
        )
    ]
    for copy in small + own_w + loads:
        copy.start()
    with phase("barrier"):
        pl.semaphore_wait(barrier, len(around))

    def ag_origin(step, way):
        return wrap(y - step if way == 0 else y + step, NY)

    def ag_copy(w, step, way, s):
        slot = 2 * ag_origin(step - 1, way) + s
        src = w_hbm[w].at[0, s] if step == 1 else wg.at[w, slot]
        return rdma(
            src, wg.at[w, slot], ag_ss.at[w, way, step - 1, s], ag_rs.at[w, way, step - 1, s],
            y_dev[way],
        )

    def ag_wait(w, step, way, s):
        here = wg.at[w, 2 * ag_origin(step, way) + s]
        rdma(
            here, here, ag_ss.at[w, way, step - 1, s], ag_rs.at[w, way, step - 1, s], y_dev[way]
        ).wait_recv()

    sends = []

    def start(copy):
        copy.start()
        sends.append(copy)

    for w in range(2):
        for s in range(2):
            for way in range(2):
                start(ag_copy(w, 1, way, s))

    for copy in small:
        copy.wait()
    for k in range(K):
        idxv[k] = jnp.where(k < cnt_hbm[0], idx_ref[0, k], NJ)
    for j in range(NJ):
        found = jnp.int32(K)
        for k in range(K):
            found = jnp.where(idxv[k] == j, k, found)
        inv[j] = found
    blank = jnp.zeros((BS, BS), BF16)
    x3[NJ] = blank
    g3[NJ] = blank
    wg[0, K] = blank
    wg[1, K] = blank

    rows = lax.broadcasted_iota(jnp.int32, (BS, BS), 0)
    cols = lax.broadcasted_iota(jnp.int32, (BS, BS), 1)
    seeds = jnp.broadcast_to(seed_ref[...], (BS, BS)).T
    mixed = scramble(seeds + (mp * BS + cols) * jnp.int32(668265261))
    keep_ref[...] = jnp.where((mixed & 7) != 0, F32(8.0 / 7.0), F32(0.0))
    half = lax.shift_right_logical(rows, 6)
    tok_x = (x + (lax.shift_right_logical(rows, 4) & 3)) & 3
    tok_z = (z + (rows & 15)) & 15
    tok_c = jnp.where(half == 1, core, 1 - core)
    token = tok_x * 32 + tok_z * 2 + tok_c
    perm_ref[...] = jnp.where(token == cols, F32(1.0), F32(0.0)).astype(BF16)

    with phase("loads"):
        for copy in loads:
            copy.wait()

    def ready_round(r):
        for shift in (1 << r, -(1 << r)):
            pl.semaphore_signal(
                ready.at[r], inc=1, device_id=z_dev(shift), device_id_type=MESH
            )

    ready_round(0)
    for k in range(K):
        x3t[k] = x3[idxv[k]].T

    def two(ref, origin):
        return ref[idxv[2 * origin]], ref[idxv[2 * origin + 1]]

    def pre_part(origin):
        left = jnp.concatenate(two(x3, origin), axis=1)
        right = wg[0, pl.ds(2 * origin, 2)].reshape(2 * BS, BS)
        return mm(left, right)

    def gd_part(origin):
        left = jnp.concatenate(two(g3, origin), axis=1)
        right = jnp.concatenate((wg[1, 2 * origin], wg[1, 2 * origin + 1]), axis=1)
        return mm_t(left, right)

    with phase("own_slots"):
        for copy in own_w:
            copy.wait()
        pre_ref[...] = pre_part(y)
        gd_ref[...] = gd_part(y)

    def ag_step(w, step):
        for s in range(2):
            for way in range(2):
                if s in ag_slots(step, way):
                    ag_wait(w, step, way, s)
                    if step < NY // 2 and s in ag_slots(step + 1, way):
                        start(ag_copy(w, step + 1, way, s))
        acc, part = ((pre_ref, pre_part), (gd_ref, gd_part))[w]
        if step < NY // 2:
            acc[...] += part(ag_origin(step, 0)) + part(ag_origin(step, 1))
        else:
            acc[...] += part(ag_origin(step, 0))

    for step in range(1, NY // 2 + 1):
        with phase(f"gather_in_{step}"):
            ag_step(0, step)
        if step <= 3:
            with phase(f"ready_{step}"):
                pl.semaphore_wait(ready.at[step - 1], 2)
            if step < 3:
                ready_round(step)
        with phase(f"gather_out_{step}"):
            ag_step(1, step)

    with phase("gelu"):
        keep = keep_ref[...]
        activation, slope = gelu_parts(pre_ref[...])
        dropped = (activation * keep).astype(BF16)
        grad_pre = (gd_ref[...] * keep * slope).astype(BF16)
        gp_ref[...] = grad_pre
        dt_ref[...] = dropped.T
        perm = perm_ref[...]
        ordered = (mm(perm, dropped).astype(BF16), mm(perm, grad_pre).astype(BF16))

    def placed(t, j, lo):
        part = ordered[t][lo:lo + 64]
        if t == 0:
            return mm(part, jnp.concatenate((wg[1, inv[j]], wg[1, inv[j + 1]]), axis=1))
        return mm_t(part, jnp.concatenate((wg[0, inv[j]], wg[0, inv[j + 1]]), axis=0))

    def c_copy(t, h):
        return rdma(c_send.at[t, h], c_recv.at[t, h], c_ss.at[t, h], c_rs.at[t, h], pair_dev)

    with phase("pair_half"):
        for t in range(2):
            for h in range(2):
                for j in range(0, HJ, 2):
                    both = placed(t, h * HJ + j, 0).astype(BF16)
                    c_send[t, h, j] = both[:, :BS]
                    c_send[t, h, j + 1] = both[:, BS:]
                start(c_copy(t, h))

    def term(w, slot):
        if w == 1:
            return mm(dt_ref[...], g3[idxv[slot]])
        return mm(x3t[slot], gp_ref[...])

    def rs_copy(w, step, way, s):
        return rdma(
            rs_send.at[w, way, step - 1, s], rs_recv.at[w, way, step - 1, s],
            rs_ss.at[w, way, step - 1, s], rs_rs.at[w, way, step - 1, s], y_dev[way],
        )

    def rs_piece(w, step, way, s):
        far = NY // 2 + 1 - step
        owner = wrap(y + far if way == 0 else y - far, NY)
        value = term(w, 2 * owner + s)
        if step > 1 and s in rs_slots(step - 1, way):
            rs_copy(w, step - 1, way, s).wait_recv()
            value = value + rs_recv[w, way, step - 2, s].astype(F32)
        rs_send[w, way, step - 1, s] = value.astype(BF16)
        start(rs_copy(w, step, way, s))

    def rs_step(step):
        for w in (1, 0):
            for s in range(2):
                for way in range(2):
                    if s in rs_slots(step, way):
                        rs_piece(w, step, way, s)

    with phase("reduce_1"):
        rs_step(1)
    with phase("own_half"):
        for t in range(2):
            for h in range(2):
                for j in range(0, HJ, 2):
                    both = placed(t, h * HJ + j, 64)
                    own[t, h, j] = both[:, :BS]
                    own[t, h, j + 1] = both[:, BS:]

    X_WAY = (0, 1, 0, 1, 0, 1)
    X_HALF = (0, 1, 1, 0, 0, 1)
    X_CHUNK = (2, 2, 1, 3, 1, 3)

    def x_copy(t, p):
        return rdma(x_send.at[t, p], x_recv.at[t, p], x_ss.at[t, p], x_rs.at[t, p], x_dev[X_WAY[p]])

    def x_own(t, h, chunk):
        span = pl.ds(chunk * 16, 16)
        return own[t, h, :, span, :] + c_recv[t, h, :, span, :].astype(F32)

    for t in range(2):
        with phase(f"pair_wait_{t}"):
            for h in range(2):
                c_copy(t, h).wait_recv()
        for p in range(4):
            x_send[t, p] = x_own(t, X_HALF[p], X_CHUNK[p]).astype(BF16)
            start(x_copy(t, p))

    with phase("reduce_2"):
        rs_step(2)

    for t in range(2):
        for p in (4, 5):
            with phase(f"x_first_{t}_{p}"):
                x_copy(t, p - 4).wait_recv()
            value = x_own(t, X_HALF[p], X_CHUNK[p]) + x_recv[t, p - 4].astype(F32)
            x_send[t, p] = value.astype(BF16)
            start(x_copy(t, p))

    with phase("reduce_3"):
        rs_step(3)

    def z_copy(t, shift):
        return rdma(
            z_send.at[t, shift], z_recv.at[t, shift], z_ss.at[t, shift], z_rs.at[t, shift],
            z_dev(shift),
        )

    for t in range(2):
        for h, (near, far) in enumerate(((3, 4), (2, 5))):
            with phase(f"x_second_{t}_{h}"):
                x_copy(t, near).wait_recv()
                x_copy(t, far).wait_recv()
            value = (
                x_own(t, h, 0) + x_recv[t, near].astype(F32) + x_recv[t, far].astype(F32)
            )
            zsum[t, pl.ds(h * HJ * 16, HJ * 16)] = value.reshape(HJ * 16, BS)
        for shift in Z_ORDER:
            z_send[t, shift] = zsum[t, pl.ds(shift, NJ, stride=16), :].astype(BF16)
            start(z_copy(t, shift))

    with phase("reduce_4"):
        rs_step(4)

    for t, o_ref in enumerate((out_ref, ing_ref)):
        total = zsum[t, pl.ds(0, NJ, stride=16), :]
        for shift in Z_ORDER:
            with phase(f"z_{t}_{shift}"):
                z_copy(t, shift).wait_recv()
            total = total + z_recv[t, shift].astype(F32)
        for j in range(NJ):
            o_ref[:, j * BS:(j + 1) * BS] = total[j:j + 1].astype(BF16)

    for w, o_ref in ((1, gwo_ref), (0, gwi_ref)):
        for s in range(2):
            value = term(w, 2 * y + s)
            for way in range(2):
                with phase(f"reduce_end_{w}_{s}_{way}"):
                    rs_copy(w, NY // 2, way, s).wait_recv()
                value = value + rs_recv[w, way, NY // 2 - 1, s].astype(F32)
            o_ref[0, s] = value

    with phase("sent"):
        for copy in sends:
            copy.wait_send()


def put_out(*refs):
    copies = [
        pltpu.make_async_copy(refs[i], refs[4 + i], refs[8].at[i]) for i in range(4)
    ]
    for copy in copies:
        copy.start()
    for copy in copies:
        copy.wait()


def body(inputs, cotangent, w_in, w_out, block_index, block_count, drop_seeds):
    vmem = pl.BlockSpec(memory_space=pltpu.VMEM)
    hbm = pl.BlockSpec(memory_space=pltpu.HBM)
    dma = pltpu.SemaphoreType.DMA
    block = (BS, BS)
    results = (
        jax.ShapeDtypeStruct((1, NJ * BS), BF16),
        jax.ShapeDtypeStruct((1, NJ * BS), BF16),
        jax.ShapeDtypeStruct((1, 2, BS, BS), F32),
        jax.ShapeDtypeStruct((1, 2, BS, BS), F32),
    )
    held = pl.pallas_call(
        kernel,
        out_shape=(
            *results,
        ),
        in_specs=[hbm] * 5 + [pl.BlockSpec(memory_space=pltpu.SMEM), hbm],
        out_specs=(vmem,) * 4,
        scratch_shapes=[
            pltpu.VMEM((NJ + 1, *block), BF16),
            pltpu.VMEM((NJ + 1, *block), BF16),
            pltpu.VMEM((K, *block), BF16),
            pltpu.VMEM((2, K + 1, *block), BF16),
            pltpu.VMEM(block, F32),
            pltpu.VMEM(block, BF16),
            pltpu.VMEM(block, F32),
            pltpu.VMEM(block, F32),
            pltpu.VMEM(block, BF16),
            pltpu.VMEM(block, BF16),
            pltpu.VMEM((2, 2, 4, 2, *block), BF16),
            pltpu.VMEM((2, 2, 4, 2, *block), BF16),
            pltpu.VMEM((2, 2, HJ, 64, BS), BF16),
            pltpu.VMEM((2, 2, HJ, 64, BS), BF16),
            pltpu.VMEM((2, 2, HJ, 64, BS), F32),
            pltpu.VMEM((2, 6, HJ, 16, BS), BF16),
            pltpu.VMEM((2, 6, HJ, 16, BS), BF16),
            pltpu.VMEM((2, NJ * 16, BS), F32),
            pltpu.VMEM((2, NZ, NJ, BS), BF16),
            pltpu.VMEM((2, NZ, NJ, BS), BF16),
            pltpu.SMEM((1, K), jnp.int32),
            pltpu.SMEM((1,), jnp.int32),
            pltpu.VMEM((1, BS), jnp.int32),
            pltpu.SMEM((K,), jnp.int32),
            pltpu.SMEM((NJ,), jnp.int32),
            dma((3,)),
            dma((2, NJ)),
            dma((2,)),
            dma((2, 2, 4, 2)),
            dma((2, 2, 4, 2)),
            dma((2, 2, 4, 2)),
            dma((2, 2, 4, 2)),
            dma((2, 2)),
            dma((2, 2)),
            dma((2, 6)),
            dma((2, 6)),
            dma((2, NZ)),
            dma((2, NZ)),
            pltpu.SemaphoreType.REGULAR((3,)),
        ],
        compiler_params=pltpu.CompilerParams(
            collective_id=0, has_side_effects=True, vmem_limit_bytes=40 << 20
        ),
    )(
        *(
            pltpu.with_memory_space_constraint(value, pltpu.HBM)
            for value in (
                inputs, cotangent, w_in, w_out, block_index
            )
        ), block_count, pltpu.with_memory_space_constraint(drop_seeds.reshape(1, BS), pltpu.HBM)
    )
    return pl.pallas_call(
        put_out,
        out_shape=results,
        in_specs=[vmem] * 4,
        out_specs=(hbm,) * 4,
        scratch_shapes=[dma((4,))],
        compiler_params=pltpu.CompilerParams(vmem_limit_bytes=1 << 20),
    )(*held)


def solution(mesh):
    placed = (
        P("dp", None),
        P("dp", None),
        P("mp", "dp", None, None),
        P("mp", "dp", None, None),
        P("mp", None),
        P("mp"),
        P("dp"),
    )
    return jax.shard_map(
        body,
        mesh=mesh,
        in_specs=placed,
        out_specs=(
            P(("dp", "mp"), None),
            P(("dp", "mp"), None),
            P("mp", "dp", None, None),
            P("mp", "dp", None, None),
        ),
        check_vma=False,
    )
```

```python
import math

import jax
import jax.numpy as jnp
from jax import lax
from jax.experimental import pallas as pl
from jax.experimental.pallas import tpu as pltpu
from jax.sharding import PartitionSpec as P

BS = 128
K = 16
NJ = 20
GROUP = 8
HALF = GROUP // 2
NG = 2 * NJ // GROUP
NY = 8
NX = 4
NZ = 16
MESH = pl.DeviceIdType.MESH
F32 = jnp.float32
BF16 = jnp.bfloat16
Z_ORDER = (8, 7, 9, 6, 10, 5, 11, 4, 12, 3, 13, 2, 14, 1, 15)


def scramble(value):
    for _ in range(2):
        value = value ^ lax.shift_right_logical(value, jnp.int32(16))
        value = value * jnp.int32(73244475)
    return value ^ lax.shift_right_logical(value, jnp.int32(16))


def gelu_parts(pre_act):
    coeff = math.sqrt(2.0 / math.pi)
    square = pre_act * pre_act
    inner = coeff * (pre_act + 0.044715 * (square * pre_act))
    tanh_val = jnp.tanh(inner)
    activation = 0.5 * pre_act * (1.0 + tanh_val)
    slope = 0.5 * (1.0 + tanh_val) + 0.5 * pre_act * (1.0 - tanh_val * tanh_val) * coeff * (
        1.0 + 3.0 * 0.044715 * square
    )
    return activation, slope


def mm(a, b):
    return lax.dot_general(a, b, (((1,), (0,)), ((), ())), preferred_element_type=F32)


def mm_t(a, b):
    return lax.dot_general(a, b, (((1,), (1,)), ((), ())), preferred_element_type=F32)


def rdma(src, dst, send_sem, recv_sem, device):
    return pltpu.make_async_remote_copy(
        src_ref=src, dst_ref=dst, send_sem=send_sem, recv_sem=recv_sem,
        device_id=device, device_id_type=MESH,
    )


def ag_slots(step, way):
    return (0, 1) if step < NY // 2 else (way,)


def rs_slots(step, way):
    return (0, 1) if step > 1 else (way,)


RS_FLAT = {
    key: i
    for i, key in enumerate(
        (step, way, s) for step in range(1, 5) for way in range(2) for s in rs_slots(step, way)
    )
}
X_WAY = (0, 1, 0, 1, 0, 1)
X_SUB = (0, 1, 1, 0, 0, 1)
X_CHUNK = (2, 2, 1, 3, 1, 3)


def kernel(
    x_hbm, g_hbm, wi_hbm, wo_hbm, idx_hbm, cnt_ref, seed_hbm,
    out_ref, ing_ref, gwi_ref, gwo_ref,
    x3, g3, x3t, wg, keep_ref, perm_ref, pre_ref, gd_ref, dt_ref, gp_ref,
    rs_send, rs_recv, c_send, c_recv, own, x_send, x_recv, zsum, z_send, z_recv,
    idx_ref, seed_ref, idxv, inv,
    sm_sem, ld_sem, wl_sem, ag_ss, ag_rs, rs_ss, rs_rs, c_ss, c_rs, x_ss, x_rs, z_ss, z_rs, ready,
):
    y = lax.axis_index("dp")
    mp = lax.axis_index("mp")
    core = lax.rem(mp, 2)
    z = lax.rem(lax.div(mp, 2), NZ)
    x = lax.div(mp, 2 * NZ)

    def at(yy, xx, zz, cc):
        return (yy, (xx * NZ + zz) * 2 + cc)

    def wrap(value, size):
        return lax.rem(value + size, size)

    y_dev = (at(wrap(y + 1, NY), x, z, core), at(wrap(y - 1, NY), x, z, core))
    x_dev = (at(y, wrap(x + 1, NX), z, core), at(y, wrap(x - 1, NX), z, core))
    pair_dev = at(y, x, z, 1 - core)

    def z_dev(shift):
        return at(y, x, wrap(z + shift, NZ), core)

    w_hbm = (wi_hbm, wo_hbm)

    barrier = pltpu.get_barrier_semaphore()
    around = (*y_dev, *x_dev, z_dev(1), z_dev(-1), pair_dev)
    for device in around:
        pl.semaphore_signal(barrier, inc=1, device_id=device, device_id_type=MESH)

    small = [
        pltpu.make_async_copy(idx_hbm, idx_ref, sm_sem.at[0]),
        pltpu.make_async_copy(seed_hbm, seed_ref, sm_sem.at[1]),
    ]
    own_w = [
        pltpu.make_async_copy(w_hbm[w].at[0], wg.at[w, pl.ds(2 * y, 2)], wl_sem.at[w])
        for w in range(2)
    ]
    for copy in small + own_w:
        copy.start()
    for j in range(NJ):
        cols = pl.ds(j * BS, BS)
        pltpu.make_async_copy(x_hbm.at[:, cols], x3.at[j], ld_sem.at[0]).start()
        pltpu.make_async_copy(g_hbm.at[:, cols], g3.at[j], ld_sem.at[1]).start()
    pl.semaphore_wait(barrier, len(around))

    def ag_origin(step, way):
        return wrap(y - step if way == 0 else y + step, NY)

    def ag_copy(w, step, way, s):
        slot = 2 * ag_origin(step - 1, way) + s
        src = w_hbm[w].at[0, s] if step == 1 else wg.at[w, slot]
        return rdma(
            src, wg.at[w, slot], ag_ss.at[w], ag_rs.at[w, way, step - 1, s], y_dev[way]
        )

    def ag_wait(w, step, way, s):
        here = wg.at[w, 2 * ag_origin(step, way) + s]
        rdma(
            here, here, ag_ss.at[w], ag_rs.at[w, way, step - 1, s], y_dev[way]
        ).wait_recv()

    for w in range(2):
        for s in range(2):
            for way in range(2):
                ag_copy(w, 1, way, s).start()

    for copy in small:
        copy.wait()
    for k in range(K):
        idxv[k] = jnp.where(k < cnt_ref[0], idx_ref[0, k], NJ)
    for j in range(NJ):
        found = jnp.int32(K)
        for k in range(K):
            found = jnp.where(idxv[k] == j, k, found)
        inv[j] = found
    blank = jnp.zeros((BS, BS), BF16)
    x3[NJ] = blank
    g3[NJ] = blank
    wg[0, K] = blank
    wg[1, K] = blank

    rows = lax.broadcasted_iota(jnp.int32, (BS, BS), 0)
    cols = lax.broadcasted_iota(jnp.int32, (BS, BS), 1)
    seeds = jnp.broadcast_to(seed_ref[...], (BS, BS)).T
    mixed = scramble(seeds + (mp * BS + cols) * jnp.int32(668265261))
    keep_ref[...] = jnp.where((mixed & 7) != 0, F32(8.0 / 7.0), F32(0.0))
    half = lax.shift_right_logical(rows, 6)
    tok_x = (x + (lax.shift_right_logical(rows, 4) & 3)) & 3
    tok_z = (z + (rows & 15)) & 15
    tok_c = jnp.where(half == 1, core, 1 - core)
    token = tok_x * 32 + tok_z * 2 + tok_c
    perm_ref[...] = jnp.where(token == cols, F32(1.0), F32(0.0)).astype(BF16)

    for i, ref in enumerate((x3, g3)):
        whole = ref.at[pl.ds(0, NJ)]
        pltpu.make_async_copy(whole, whole, ld_sem.at[i]).wait()

    def ready_round(r):
        for shift in (1 << r, -(1 << r)):
            pl.semaphore_signal(
                ready.at[r], inc=1, device_id=z_dev(shift), device_id_type=MESH
            )

    ready_round(0)

    def two(ref, origin):
        return ref[idxv[2 * origin]], ref[idxv[2 * origin + 1]]

    def pre_part(origin):
        left = jnp.concatenate(two(x3, origin), axis=1)
        right = wg[0, pl.ds(2 * origin, 2)].reshape(2 * BS, BS)
        return mm(left, right)

    def gd_part(origin):
        left = jnp.concatenate(two(g3, origin), axis=1)
        right = jnp.concatenate((wg[1, 2 * origin], wg[1, 2 * origin + 1]), axis=1)
        return mm_t(left, right)

    for copy in own_w:
        copy.wait()

    def ag_step(w, step):
        for s in range(2):
            for way in range(2):
                if s in ag_slots(step, way):
                    ag_wait(w, step, way, s)
                    if step < NY // 2 and s in ag_slots(step + 1, way):
                        ag_copy(w, step + 1, way, s).start()

    pre_ref[...] = pre_part(y)
    gd_ref[...] = gd_part(y)
    for step in range(1, NY // 2):
        ag_step(0, step)
        ag_step(1, step)
        pl.semaphore_wait(ready.at[step - 1], 2)
        if step < 3:
            ready_round(step)
        if step == 1:
            for k in range(K):
                x3t[k] = x3[idxv[k]].T
        left, right = ag_origin(step, 0), ag_origin(step, 1)
        pre_ref[...] += pre_part(left) + pre_part(right)
        gd_ref[...] += gd_part(left) + gd_part(right)

    perm = perm_ref[...]
    keep = keep_ref[...]
    far = ag_origin(NY // 2, 0)
    ag_step(0, NY // 2)
    activation, slope = gelu_parts(pre_ref[...] + pre_part(far))
    dropped = (activation * keep).astype(BF16)
    slope = slope * keep
    dt_ref[...] = dropped.T
    first = mm(perm, dropped).astype(BF16)
    ag_step(1, NY // 2)
    grad_pre = ((gd_ref[...] + gd_part(far)) * slope).astype(BF16)
    gp_ref[...] = grad_pre
    ordered = (first, mm(perm, grad_pre).astype(BF16))

    def placed(u, lo):
        t, j = divmod(u, NJ)
        part = ordered[t][lo:lo + 64]
        if t == 0:
            return mm(part, jnp.concatenate((wg[1, inv[j]], wg[1, inv[j + 1]]), axis=1))
        return mm_t(part, jnp.concatenate((wg[0, inv[j]], wg[0, inv[j + 1]]), axis=0))

    def fill(ref, g, lo):
        for i in range(0, GROUP, 2):
            both = placed(g * GROUP + i, lo).astype(ref.dtype)
            ref[g, i] = both[:, :BS]
            ref[g, i + 1] = both[:, BS:]

    def c_copy(g):
        return rdma(c_send.at[g], c_recv.at[g], c_ss, c_rs.at[g], pair_dev)

    def pair_out(g):
        fill(c_send, g, 0)
        c_copy(g).start()

    def term(w, slot):
        if w == 1:
            return mm(dt_ref[...], g3[idxv[slot]])
        return mm(x3t[slot], gp_ref[...])

    def rs_copy(w, step, way, s):
        i = RS_FLAT[step, way, s]
        return rdma(rs_send.at[w, i], rs_recv.at[w, i], rs_ss.at[w], rs_rs.at[w, i], y_dev[way])

    def rs_piece(w, step, way, s):
        far = NY // 2 + 1 - step
        owner = wrap(y + far if way == 0 else y - far, NY)
        value = term(w, 2 * owner + s)
        if step > 1 and s in rs_slots(step - 1, way):
            rs_copy(w, step - 1, way, s).wait_recv()
            value = value + rs_recv[w, RS_FLAT[step - 1, way, s]].astype(F32)
        rs_send[w, RS_FLAT[step, way, s]] = value.astype(BF16)
        rs_copy(w, step, way, s).start()

    def rs_both(w, step, chain):
        for way in range(2):
            rs_piece(w, step, way, way ^ chain)

    def rs_end(w, s):
        value = term(w, 2 * y + s)
        for way in range(2):
            rs_copy(w, NY // 2, way, s).wait_recv()
            value = value + rs_recv[w, RS_FLAT[NY // 2, way, s]].astype(F32)
        (gwi_ref, gwo_ref)[w][0, s] = value

    def x_copy(g, p):
        sem = x_rs.at[g, min(p, 2)]
        return rdma(x_send.at[g, p], x_recv.at[g, p], x_ss, sem, x_dev[X_WAY[p]])

    def x_own(g, sub, chunk):
        some, span = pl.ds(sub * HALF, HALF), pl.ds(chunk * 16, 16)
        return own[g, some, span, :] + c_recv[g, some, span, :].astype(F32)

    def x_first(g):
        c_copy(g).wait_recv()
        for p in range(4):
            x_send[g, p] = x_own(g, X_SUB[p], X_CHUNK[p]).astype(BF16)
            x_copy(g, p).start()

    def x_second(g):
        for p in (4, 5):
            x_copy(g, p - 4).wait_recv()
            value = x_own(g, X_SUB[p], X_CHUNK[p]) + x_recv[g, p - 4].astype(F32)
            x_send[g, p] = value.astype(BF16)
            x_copy(g, p).start()

    def z_first(g):
        last = pl.ds(2, 4)
        rdma(x_send.at[g, last], x_recv.at[g, last], x_ss, x_rs.at[g, 2], x_dev[0]).wait_recv()
        for sub, (near, more) in enumerate(((3, 4), (2, 5))):
            value = x_own(g, sub, 0) + x_recv[g, near].astype(F32) + x_recv[g, more].astype(F32)
            zsum[g, pl.ds(sub * HALF * NZ, HALF * NZ)] = value.reshape(HALF * NZ, BS)
        for shift in Z_ORDER:
            z_send[g, shift] = zsum[g, pl.ds(shift, GROUP, stride=NZ), :].astype(BF16)
            rdma(
                z_send.at[g, shift], z_recv.at[g, shift], z_ss, z_rs.at[g], z_dev(shift)
            ).start()

    others = pl.ds(1, NZ - 1)

    def z_end(g):
        rdma(
            z_send.at[g, others], z_recv.at[g, others], z_ss, z_rs.at[g], z_dev(1)
        ).wait_recv()
        total = zsum[g, pl.ds(0, GROUP, stride=NZ), :]
        for shift in Z_ORDER:
            total = total + z_recv[g, shift].astype(F32)
        for i in range(GROUP):
            t, j = divmod(g * GROUP + i, NJ)
            (out_ref, ing_ref)[t][:, j * BS:(j + 1) * BS] = total[i:i + 1].astype(BF16)

    pair_out(0)
    for w in (1, 0):
        rs_both(w, 1, 0)
    pair_out(1)
    for w in (1, 0):
        rs_both(w, 2, 1)
    for g in range(2, NG):
        pair_out(g)
    for g in range(NG):
        fill(own, g, 64)
    x_first(0)
    x_first(1)
    rs_both(1, 2, 0)
    x_first(2)
    rs_both(0, 2, 0)
    x_second(0)
    x_first(3)
    rs_both(1, 3, 1)
    x_second(1)
    x_first(4)
    rs_both(0, 3, 1)
    x_second(2)
    rs_both(1, 3, 0)
    z_first(0)
    rs_both(0, 3, 0)
    x_second(3)
    z_first(1)
    rs_both(1, 4, 1)
    x_second(4)
    z_first(2)
    rs_both(0, 4, 1)
    rs_both(1, 4, 0)
    z_first(3)
    rs_both(0, 4, 0)
    z_first(4)
    for w in (1, 0):
        rs_end(w, 0)
        rs_end(w, 1)
    for g in range(NG):
        z_end(g)

    for w in range(2):
        here = wg.at[w, pl.ds(0, 14)]
        rdma(here, here, ag_ss.at[w], ag_rs.at[w, 0, 0, 0], y_dev[0]).wait_send()
        rdma(rs_send.at[w], rs_recv.at[w], rs_ss.at[w], rs_rs.at[w, 0], y_dev[0]).wait_send()
    rdma(c_send, c_recv, c_ss, c_rs.at[0], pair_dev).wait_send()
    rdma(x_send, x_recv, x_ss, x_rs.at[0, 0], x_dev[0]).wait_send()
    rdma(
        z_send.at[:, others], z_recv.at[:, others], z_ss, z_rs.at[0], z_dev(1)
    ).wait_send()


def put_out(*refs):
    copies = [
        pltpu.make_async_copy(refs[i], refs[4 + i], refs[8].at[i]) for i in range(4)
    ]
    for copy in copies:
        copy.start()
    for copy in copies:
        copy.wait()


def body(inputs, cotangent, w_in, w_out, block_index, block_count, drop_seeds):
    vmem = pl.BlockSpec(memory_space=pltpu.VMEM)
    hbm = pl.BlockSpec(memory_space=pltpu.HBM)
    dma = pltpu.SemaphoreType.DMA
    block = (BS, BS)
    results = (
        jax.ShapeDtypeStruct((1, NJ * BS), BF16),
        jax.ShapeDtypeStruct((1, NJ * BS), BF16),
        jax.ShapeDtypeStruct((1, 2, BS, BS), F32),
        jax.ShapeDtypeStruct((1, 2, BS, BS), F32),
    )
    held = pl.pallas_call(
        kernel,
        out_shape=(
            *results,
        ),
        in_specs=[hbm] * 5 + [pl.BlockSpec(memory_space=pltpu.SMEM), hbm],
        out_specs=(vmem,) * 4,
        scratch_shapes=[
            pltpu.VMEM((NJ + 1, *block), BF16),
            pltpu.VMEM((NJ + 1, *block), BF16),
            pltpu.VMEM((K, *block), BF16),
            pltpu.VMEM((2, K + 1, *block), BF16),
            pltpu.VMEM(block, F32),
            pltpu.VMEM(block, BF16),
            pltpu.VMEM(block, F32),
            pltpu.VMEM(block, F32),
            pltpu.VMEM(block, BF16),
            pltpu.VMEM(block, BF16),
            pltpu.VMEM((2, 14, *block), BF16),
            pltpu.VMEM((2, 14, *block), BF16),
            pltpu.VMEM((NG, GROUP, 64, BS), BF16),
            pltpu.VMEM((NG, GROUP, 64, BS), BF16),
            pltpu.VMEM((NG, GROUP, 64, BS), F32),
            pltpu.VMEM((NG, 6, HALF, 16, BS), BF16),
            pltpu.VMEM((NG, 6, HALF, 16, BS), BF16),
            pltpu.VMEM((NG, GROUP * NZ, BS), F32),
            pltpu.VMEM((NG, NZ, GROUP, BS), BF16),
            pltpu.VMEM((NG, NZ, GROUP, BS), BF16),
            pltpu.SMEM((1, K), jnp.int32),
            pltpu.VMEM((1, BS), jnp.int32),
            pltpu.SMEM((K,), jnp.int32),
            pltpu.SMEM((NJ,), jnp.int32),
            dma((2,)),
            dma((2,)),
            dma((2,)),
            dma((2,)),
            dma((2, 2, 4, 2)),
            dma((2,)),
            dma((2, 14)),
            dma(()),
            dma((NG,)),
            dma(()),
            dma((NG, 3)),
            dma(()),
            dma((NG,)),
            pltpu.SemaphoreType.REGULAR((3,)),
        ],
        compiler_params=pltpu.CompilerParams(
            collective_id=0, has_side_effects=True, vmem_limit_bytes=40 << 20
        ),
    )(
        *(
            pltpu.with_memory_space_constraint(value, pltpu.HBM)
            for value in (
                inputs, cotangent, w_in, w_out, block_index
            )
        ), block_count, pltpu.with_memory_space_constraint(drop_seeds.reshape(1, BS), pltpu.HBM)
    )
    return pl.pallas_call(
        put_out,
        out_shape=results,
        in_specs=[vmem] * 4,
        out_specs=(hbm,) * 4,
        scratch_shapes=[dma((4,))],
        compiler_params=pltpu.CompilerParams(vmem_limit_bytes=1 << 20),
    )(*held)


def solution(mesh):
    placed = (
        P("dp", None),
        P("dp", None),
        P("mp", "dp", None, None),
        P("mp", "dp", None, None),
        P("mp", None),
        P("mp"),
        P("dp"),
    )
    return jax.shard_map(
        body,
        mesh=mesh,
        in_specs=placed,
        out_specs=(
            P(("dp", "mp"), None),
            P(("dp", "mp"), None),
            P("mp", "dp", None, None),
            P("mp", "dp", None, None),
        ),
        check_vma=False,
    )
```

```python
import math

import jax
import jax.numpy as jnp
from jax import lax
from jax.experimental import pallas as pl
from jax.experimental.pallas import tpu as pltpu
from jax.sharding import PartitionSpec as P

BS = 128
K = 16
NJ = 20
GROUP = 8
HALF = GROUP // 2
NG = 2 * NJ // GROUP
NY = 8
NX = 4
NZ = 16
MESH = pl.DeviceIdType.MESH
F32 = jnp.float32
BF16 = jnp.bfloat16
Z_ORDER = (8, 7, 9, 6, 10, 5, 11, 4, 12, 3, 13, 2, 14, 1, 15)


def scramble(value):
    for _ in range(2):
        value = value ^ lax.shift_right_logical(value, jnp.int32(16))
        value = value * jnp.int32(73244475)
    return value ^ lax.shift_right_logical(value, jnp.int32(16))


def gelu_parts(pre_act):
    coeff = math.sqrt(2.0 / math.pi)
    square = pre_act * pre_act
    inner = coeff * (pre_act + 0.044715 * (square * pre_act))
    tanh_val = jnp.tanh(inner)
    activation = 0.5 * pre_act * (1.0 + tanh_val)
    slope = 0.5 * (1.0 + tanh_val) + 0.5 * pre_act * (1.0 - tanh_val * tanh_val) * coeff * (
        1.0 + 3.0 * 0.044715 * square
    )
    return activation, slope


def mm(a, b):
    return lax.dot_general(a, b, (((1,), (0,)), ((), ())), preferred_element_type=F32)


def mm_t(a, b):
    return lax.dot_general(a, b, (((1,), (1,)), ((), ())), preferred_element_type=F32)


def rdma(src, dst, send_sem, recv_sem, device):
    return pltpu.make_async_remote_copy(
        src_ref=src, dst_ref=dst, send_sem=send_sem, recv_sem=recv_sem,
        device_id=device, device_id_type=MESH,
    )


def ag_slots(step, way):
    return (0, 1) if step < NY // 2 else (way,)


def rs_slots(step, way):
    return (0, 1) if step > 1 else (way,)


RS_FLAT = {
    key: i
    for i, key in enumerate(
        (step, way, s) for step in range(1, 5) for way in range(2) for s in rs_slots(step, way)
    )
}
X_WAY = (0, 1, 0, 1, 0, 1)
X_SUB = (0, 1, 1, 0, 0, 1)
X_CHUNK = (2, 2, 1, 3, 1, 3)


def kernel(
    x_hbm, g_hbm, wi_hbm, wo_hbm, idx_hbm, cnt_ref, seed_hbm,
    out_ref, ing_ref, gwi_ref, gwo_ref,
    x3, g3, x3t, wg, keep_ref, perm_ref, pre_ref, gd_ref, dt_ref, gp_ref,
    wp, ex_send, ex_recv, rs_send, rs_recv, own, x_send, x_recv, zsum, z_send, z_recv,
    idx_ref, seed_ref, idxv, inv, idxp, invp,
    sm_sem, ld_sem, wl_sem, ag_ss, ag_rs, wp_ss, wp_rs, id_sem, ex_ss, ex_rs, rs_ss, rs_rs, x_ss, x_rs, z_ss, z_rs, ready,
):
    y = lax.axis_index("dp")
    mp = lax.axis_index("mp")
    core = lax.rem(mp, 2)
    z = lax.rem(lax.div(mp, 2), NZ)
    x = lax.div(mp, 2 * NZ)

    def at(yy, xx, zz, cc):
        return (yy, (xx * NZ + zz) * 2 + cc)

    def wrap(value, size):
        return lax.rem(value + size, size)

    y_dev = (at(wrap(y + 1, NY), x, z, core), at(wrap(y - 1, NY), x, z, core))
    x_dev = (at(y, wrap(x + 1, NX), z, core), at(y, wrap(x - 1, NX), z, core))
    pair_dev = at(y, x, z, 1 - core)

    def z_dev(shift):
        return at(y, x, wrap(z + shift, NZ), core)

    w_hbm = (wi_hbm, wo_hbm)

    barrier = pltpu.get_barrier_semaphore()
    around = (*y_dev, *x_dev, z_dev(1), z_dev(-1), pair_dev)
    for device in around:
        pl.semaphore_signal(barrier, inc=1, device_id=device, device_id_type=MESH)

    small = [
        pltpu.make_async_copy(idx_hbm, idx_ref, sm_sem.at[0]),
        pltpu.make_async_copy(seed_hbm, seed_ref, sm_sem.at[1]),
    ]
    own_w = [
        pltpu.make_async_copy(w_hbm[w].at[0], wg.at[w, pl.ds(2 * y, 2)], wl_sem.at[w])
        for w in range(2)
    ]
    for copy in small + own_w:
        copy.start()
    for j in range(NJ):
        cols = pl.ds(j * BS, BS)
        pltpu.make_async_copy(x_hbm.at[:, cols], x3.at[j], ld_sem.at[0]).start()
        pltpu.make_async_copy(g_hbm.at[:, cols], g3.at[j], ld_sem.at[1]).start()
    pl.semaphore_wait(barrier, len(around))

    def ag_origin(step, way):
        return wrap(y - step if way == 0 else y + step, NY)

    def ag_copy(w, step, way, s):
        hops = 2 if step == NY // 2 else 1
        slot = 2 * ag_origin(step - hops, way) + s
        src = w_hbm[w].at[0, s] if step == 1 else wg.at[w, slot]
        device = at(ag_origin(hops, 1 - way), x, z, core)
        return rdma(src, wg.at[w, slot], ag_ss.at[w], ag_rs.at[w, way, step - 1, s], device)

    def ag_wait(w, step, way, s):
        here = wg.at[w, 2 * ag_origin(step, way) + s]
        rdma(
            here, here, ag_ss.at[w], ag_rs.at[w, way, step - 1, s], y_dev[way]
        ).wait_recv()

    def pass_on(w, slot):
        return rdma(wg.at[w, slot], wp.at[w, slot], wp_ss.at[w], wp_rs.at[w], pair_dev)

    for w in range(2):
        for s in range(2):
            for way in range(2):
                ag_copy(w, 1, way, s).start()
        rdma(
            w_hbm[w].at[0], wp.at[w, pl.ds(2 * y, 2)], wp_ss.at[w], wp_rs.at[w], pair_dev
        ).start()

    for copy in small:
        copy.wait()
    for k in range(K):
        idxv[k] = jnp.where(k < cnt_ref[0], idx_ref[0, k], NJ)
    tables = rdma(idxv, idxp, id_sem.at[0], id_sem.at[1], pair_dev)
    tables.start()

    def invert(src, dst):
        for j in range(NJ):
            found = jnp.int32(K)
            for k in range(K):
                found = jnp.where(src[k] == j, k, found)
            dst[j] = found

    invert(idxv, inv)
    blank = jnp.zeros((BS, BS), BF16)
    x3[NJ] = blank
    g3[NJ] = blank
    wg[0, K] = blank
    wg[1, K] = blank
    wp[0, K] = blank
    wp[1, K] = blank

    rows = lax.broadcasted_iota(jnp.int32, (BS, BS), 0)
    cols = lax.broadcasted_iota(jnp.int32, (BS, BS), 1)
    seeds = jnp.broadcast_to(seed_ref[...], (BS, BS)).T
    mixed = scramble(seeds + (mp * BS + cols) * jnp.int32(668265261))
    keep_ref[...] = jnp.where((mixed & 7) != 0, F32(8.0 / 7.0), F32(0.0))
    half = lax.shift_right_logical(rows, 6)
    tok_x = (x + (lax.shift_right_logical(rows, 4) & 3)) & 3
    tok_z = (z + (rows & 15)) & 15
    tok_c = jnp.where(half == 1, core, 1 - core)
    token = tok_x * 32 + tok_z * 2 + tok_c
    perm_ref[...] = jnp.where(token == cols, F32(1.0), F32(0.0)).astype(BF16)

    for i, ref in enumerate((x3, g3)):
        whole = ref.at[pl.ds(0, NJ)]
        pltpu.make_async_copy(whole, whole, ld_sem.at[i]).wait()

    def ready_round(r):
        for shift in (1 << r, -(1 << r)):
            pl.semaphore_signal(
                ready.at[r], inc=1, device_id=z_dev(shift), device_id_type=MESH
            )

    ready_round(0)

    def two(ref, origin):
        return ref[idxv[2 * origin]], ref[idxv[2 * origin + 1]]

    def pre_part(origin):
        left = jnp.concatenate(two(x3, origin), axis=1)
        right = wg[0, pl.ds(2 * origin, 2)].reshape(2 * BS, BS)
        return mm(left, right)

    def gd_part(origin):
        left = jnp.concatenate(two(g3, origin), axis=1)
        right = jnp.concatenate((wg[1, 2 * origin], wg[1, 2 * origin + 1]), axis=1)
        return mm_t(left, right)

    for copy in own_w:
        copy.wait()

    def ag_step(w, step):
        for s in range(2):
            for way in range(2):
                if s in ag_slots(step, way):
                    ag_wait(w, step, way, s)
                    if step + 1 < NY // 2:
                        ag_copy(w, step + 1, way, s).start()
                    pass_on(w, 2 * ag_origin(step, way) + s).start()
        if step == NY // 2 - 2:
            for way in range(2):
                ag_copy(w, NY // 2, way, way).start()

    pre_ref[...] = pre_part(y)
    gd_ref[...] = gd_part(y)
    for step in range(1, NY // 2):
        ag_step(0, step)
        ag_step(1, step)
        pl.semaphore_wait(ready.at[step - 1], 2)
        if step < 3:
            ready_round(step)
        if step == 1:
            for k in range(K):
                x3t[k] = x3[idxv[k]].T
        if step == 2:
            tables.wait()
            invert(idxp, invp)
        left, right = ag_origin(step, 0), ag_origin(step, 1)
        pre_ref[...] += pre_part(left) + pre_part(right)
        gd_ref[...] += gd_part(left) + gd_part(right)

    def swap(t):
        return rdma(ex_send.at[t], ex_recv.at[t], ex_ss, ex_rs.at[t], pair_dev)

    perm = perm_ref[...]
    keep = keep_ref[...]
    far = ag_origin(NY // 2, 0)
    ag_step(0, NY // 2)
    activation, slope = gelu_parts(pre_ref[...] + pre_part(far))
    dropped = (activation * keep).astype(BF16)
    slope = slope * keep
    dt_ref[...] = dropped.T
    ordered = mm(perm, dropped).astype(BF16)
    ex_send[0] = ordered[:64]
    mine = [ordered[64:]]
    swap(0).start()

    def term(w, slot):
        if w == 1:
            return mm(dt_ref[...], g3[idxv[slot]])
        return mm(x3t[slot], gp_ref[...])

    def rs_copy(w, step, way, s):
        i = RS_FLAT[step, way, s]
        return rdma(rs_send.at[w, i], rs_recv.at[w, i], rs_ss.at[w], rs_rs.at[w, i], y_dev[way])

    def rs_piece(w, step, way, s):
        far = NY // 2 + 1 - step
        owner = wrap(y + far if way == 0 else y - far, NY)
        value = term(w, 2 * owner + s)
        if step > 1 and s in rs_slots(step - 1, way):
            rs_copy(w, step - 1, way, s).wait_recv()
            value = value + rs_recv[w, RS_FLAT[step - 1, way, s]].astype(F32)
        rs_send[w, RS_FLAT[step, way, s]] = value.astype(BF16)
        rs_copy(w, step, way, s).start()

    def rs_both(w, step, chain):
        for way in range(2):
            rs_piece(w, step, way, way ^ chain)

    def rs_end(w, s):
        value = term(w, 2 * y + s)
        for way in range(2):
            rs_copy(w, NY // 2, way, s).wait_recv()
            value = value + rs_recv[w, RS_FLAT[NY // 2, way, s]].astype(F32)
        (gwi_ref, gwo_ref)[w][0, s] = value

    rs_both(1, 1, 0)
    ag_step(1, NY // 2)
    grad_pre = ((gd_ref[...] + gd_part(far)) * slope).astype(BF16)
    gp_ref[...] = grad_pre
    ordered = mm(perm, grad_pre).astype(BF16)
    ex_send[1] = ordered[:64]
    mine.append(ordered[64:])
    swap(1).start()

    def x_copy(g, p):
        sem = x_rs.at[g, min(p, 2)]
        return rdma(x_send.at[g, p], x_recv.at[g, p], x_ss, sem, x_dev[X_WAY[p]])

    def x_own(g, sub, chunk):
        return own[g, pl.ds(sub * HALF, HALF), pl.ds(chunk * 16, 16), :]

    def x_first(g, pieces):
        for p in pieces:
            x_send[g, p] = x_own(g, X_SUB[p], X_CHUNK[p]).astype(BF16)
            x_copy(g, p).start()

    def x_second(g):
        for p in (4, 5):
            x_copy(g, p - 4).wait_recv()
            value = x_own(g, X_SUB[p], X_CHUNK[p]) + x_recv[g, p - 4].astype(F32)
            x_send[g, p] = value.astype(BF16)
            x_copy(g, p).start()

    def z_first(g):
        last = pl.ds(2, 4)
        rdma(x_send.at[g, last], x_recv.at[g, last], x_ss, x_rs.at[g, 2], x_dev[0]).wait_recv()
        for sub, (near, more) in enumerate(((3, 4), (2, 5))):
            value = x_own(g, sub, 0) + x_recv[g, near].astype(F32) + x_recv[g, more].astype(F32)
            zsum[g, pl.ds(sub * HALF * NZ, HALF * NZ)] = value.reshape(HALF * NZ, BS)
        for shift in Z_ORDER:
            z_send[g, shift] = zsum[g, pl.ds(shift, GROUP, stride=NZ), :].astype(BF16)
            rdma(
                z_send.at[g, shift], z_recv.at[g, shift], z_ss, z_rs.at[g], z_dev(shift)
            ).start()

    others = pl.ds(1, NZ - 1)

    def z_end(g):
        rdma(
            z_send.at[g, others], z_recv.at[g, others], z_ss, z_rs.at[g], z_dev(1)
        ).wait_recv()
        total = zsum[g, pl.ds(0, GROUP, stride=NZ), :]
        for shift in Z_ORDER:
            total = total + z_recv[g, shift].astype(F32)
        for i in range(GROUP):
            t, j = divmod(g * GROUP + i, NJ)
            (out_ref, ing_ref)[t][:, j * BS:(j + 1) * BS] = total[i:i + 1].astype(BF16)

    both = []

    def product(u):
        t, j = divmod(u, NJ)

        def pair(j):
            w = 1 - t
            return jnp.concatenate((wg[w, inv[j]], wp[w, invp[j]]), axis=t)

        right = jnp.concatenate((pair(j), pair(j + 1)), axis=1 - t)
        return (mm, mm_t)[t](both[t], right)

    def fill(g):
        for i in range(0, GROUP, 2):
            value = product(g * GROUP + i)
            own[g, i] = value[:, :BS]
            own[g, i + 1] = value[:, BS:]

    for w in range(2):
        here = wp.at[w, pl.ds(0, K)]
        rdma(here, here, wp_ss.at[w], wp_rs.at[w], pair_dev).wait_recv()

    def swap_end(t):
        swap(t).wait_recv()
        both.append(jnp.concatenate((mine[t], ex_recv[t]), axis=1))

    rs_both(0, 1, 0)
    swap_end(0)
    fill(0)
    x_first(0, (0, 1))
    fill(1)
    x_first(1, (0, 1))
    swap_end(1)
    for g in range(2, NG):
        fill(g)
        x_first(g, (0, 1))
    rs_both(1, 2, 1)
    rs_both(0, 2, 1)
    for g in range(NG):
        x_first(g, (2, 3))
    rs_both(1, 2, 0)
    x_second(0)
    rs_both(0, 2, 0)
    x_second(1)
    x_second(2)
    rs_both(1, 3, 1)
    x_second(3)
    x_second(4)
    rs_both(0, 3, 1)
    z_first(0)
    rs_both(1, 3, 0)
    z_first(1)
    rs_both(0, 3, 0)
    z_first(2)
    rs_both(1, 4, 1)
    z_first(3)
    rs_both(0, 4, 1)
    z_first(4)
    rs_both(1, 4, 0)
    rs_both(0, 4, 0)
    for w in (1, 0):
        rs_end(w, 1)
        rs_end(w, 0)
    for g in range(NG):
        z_end(g)

    for w in range(2):
        here = wg.at[w, pl.ds(0, 14)]
        rdma(here, here, ag_ss.at[w], ag_rs.at[w, 0, 0, 0], y_dev[0]).wait_send()
        rdma(rs_send.at[w], rs_recv.at[w], rs_ss.at[w], rs_rs.at[w, 0], y_dev[0]).wait_send()
        here = wg.at[w, pl.ds(0, K)]
        rdma(here, here, wp_ss.at[w], wp_rs.at[w], pair_dev).wait_send()
    rdma(ex_send, ex_recv, ex_ss, ex_rs.at[0], pair_dev).wait_send()
    rdma(x_send, x_recv, x_ss, x_rs.at[0, 0], x_dev[0]).wait_send()
    rdma(
        z_send.at[:, others], z_recv.at[:, others], z_ss, z_rs.at[0], z_dev(1)
    ).wait_send()


def put_out(*refs):
    copies = [
        pltpu.make_async_copy(refs[i], refs[4 + i], refs[8].at[i]) for i in range(4)
    ]
    for copy in copies:
        copy.start()
    for copy in copies:
        copy.wait()


def body(inputs, cotangent, w_in, w_out, block_index, block_count, drop_seeds):
    vmem = pl.BlockSpec(memory_space=pltpu.VMEM)
    hbm = pl.BlockSpec(memory_space=pltpu.HBM)
    dma = pltpu.SemaphoreType.DMA
    block = (BS, BS)
    results = (
        jax.ShapeDtypeStruct((1, NJ * BS), BF16),
        jax.ShapeDtypeStruct((1, NJ * BS), BF16),
        jax.ShapeDtypeStruct((1, 2, BS, BS), F32),
        jax.ShapeDtypeStruct((1, 2, BS, BS), F32),
    )
    held = pl.pallas_call(
        kernel,
        out_shape=(
            *results,
        ),
        in_specs=[hbm] * 5 + [pl.BlockSpec(memory_space=pltpu.SMEM), hbm],
        out_specs=(vmem,) * 4,
        scratch_shapes=[
            pltpu.VMEM((NJ + 1, *block), BF16),
            pltpu.VMEM((NJ + 1, *block), BF16),
            pltpu.VMEM((K, *block), BF16),
            pltpu.VMEM((2, K + 1, *block), BF16),
            pltpu.VMEM(block, F32),
            pltpu.VMEM(block, BF16),
            pltpu.VMEM(block, F32),
            pltpu.VMEM(block, F32),
            pltpu.VMEM(block, BF16),
            pltpu.VMEM(block, BF16),
            pltpu.VMEM((2, K + 1, *block), BF16),
            pltpu.VMEM((2, 64, BS), BF16),
            pltpu.VMEM((2, 64, BS), BF16),
            pltpu.VMEM((2, 14, *block), BF16),
            pltpu.VMEM((2, 14, *block), BF16),
            pltpu.VMEM((NG, GROUP, 64, BS), F32),
            pltpu.VMEM((NG, 6, HALF, 16, BS), BF16),
            pltpu.VMEM((NG, 6, HALF, 16, BS), BF16),
            pltpu.VMEM((NG, GROUP * NZ, BS), F32),
            pltpu.VMEM((NG, NZ, GROUP, BS), BF16),
            pltpu.VMEM((NG, NZ, GROUP, BS), BF16),
            pltpu.SMEM((1, K), jnp.int32),
            pltpu.VMEM((1, BS), jnp.int32),
            pltpu.SMEM((K,), jnp.int32),
            pltpu.SMEM((NJ,), jnp.int32),
            pltpu.SMEM((K,), jnp.int32),
            pltpu.SMEM((NJ,), jnp.int32),
            dma((2,)),
            dma((2,)),
            dma((2,)),
            dma((2,)),
            dma((2, 2, 4, 2)),
            dma((2,)),
            dma((2,)),
            dma((2,)),
            dma(()),
            dma((2,)),
            dma((2,)),
            dma((2, 14)),
            dma(()),
            dma((NG, 3)),
            dma(()),
            dma((NG,)),
            pltpu.SemaphoreType.REGULAR((3,)),
        ],
        compiler_params=pltpu.CompilerParams(
            collective_id=0, has_side_effects=True, vmem_limit_bytes=40 << 20
        ),
    )(
        *(
            pltpu.with_memory_space_constraint(value, pltpu.HBM)
            for value in (
                inputs, cotangent, w_in, w_out, block_index
            )
        ), block_count, pltpu.with_memory_space_constraint(drop_seeds.reshape(1, BS), pltpu.HBM)
    )
    return pl.pallas_call(
        put_out,
        out_shape=results,
        in_specs=[vmem] * 4,
        out_specs=(hbm,) * 4,
        scratch_shapes=[dma((4,))],
        compiler_params=pltpu.CompilerParams(vmem_limit_bytes=1 << 20),
    )(*held)


def solution(mesh):
    placed = (
        P("dp", None),
        P("dp", None),
        P("mp", "dp", None, None),
        P("mp", "dp", None, None),
        P("mp", None),
        P("mp"),
        P("dp"),
    )
    return jax.shard_map(
        body,
        mesh=mesh,
        in_specs=placed,
        out_specs=(
            P(("dp", "mp"), None),
            P(("dp", "mp"), None),
            P("mp", "dp", None, None),
            P("mp", "dp", None, None),
        ),
        check_vma=False,
    )
```

```python
import math

import jax
import jax.numpy as jnp
from jax import lax
from jax.experimental import pallas as pl
from jax.experimental.pallas import tpu as pltpu
from jax.sharding import PartitionSpec as P

BS = 128
K = 16
NJ = 20
GROUP = 8
HALF = GROUP // 2
NG = 2 * NJ // GROUP
NY = 8
NX = 4
NZ = 16
MESH = pl.DeviceIdType.MESH
F32 = jnp.float32
BF16 = jnp.bfloat16
Z_ORDER = (8, 7, 9, 6, 10, 5, 11, 4, 12, 3, 13, 2, 14, 1, 15)


def scramble(value):
    for _ in range(2):
        value = value ^ lax.shift_right_logical(value, jnp.int32(16))
        value = value * jnp.int32(73244475)
    return value ^ lax.shift_right_logical(value, jnp.int32(16))


def gelu_parts(pre_act):
    coeff = math.sqrt(2.0 / math.pi)
    square = pre_act * pre_act
    inner = coeff * (pre_act + 0.044715 * (square * pre_act))
    tanh_val = jnp.tanh(inner)
    activation = 0.5 * pre_act * (1.0 + tanh_val)
    slope = 0.5 * (1.0 + tanh_val) + 0.5 * pre_act * (1.0 - tanh_val * tanh_val) * coeff * (
        1.0 + 3.0 * 0.044715 * square
    )
    return activation, slope


def mm(a, b):
    return lax.dot_general(a, b, (((1,), (0,)), ((), ())), preferred_element_type=F32)


def mm_t(a, b):
    return lax.dot_general(a, b, (((1,), (1,)), ((), ())), preferred_element_type=F32)


def rdma(src, dst, send_sem, recv_sem, device):
    return pltpu.make_async_remote_copy(
        src_ref=src, dst_ref=dst, send_sem=send_sem, recv_sem=recv_sem,
        device_id=device, device_id_type=MESH,
    )


def ag_slots(step, way):
    return (0, 1) if step < NY // 2 else (way,)


def rs_slots(step, way):
    return (0, 1) if step > 1 else (way,)


RS_FLAT = {
    key: i
    for i, key in enumerate(
        (step, way, s) for step in range(1, 5) for way in range(2) for s in rs_slots(step, way)
    )
}
X_WAY = (0, 1, 0, 1, 0, 1)
X_SUB = (0, 1, 1, 0, 0, 1)
X_CHUNK = (2, 2, 1, 3, 1, 3)


def kernel(
    x_hbm, g_hbm, wi_hbm, wo_hbm, idx_hbm, cnt_ref, seed_hbm,
    out_ref, ing_ref, gwi_ref, gwo_ref,
    x3, g3, x3t, wg, keep_ref, perm_ref, pre_ref, gd_ref, dt_ref, gp_ref,
    wp, ex_send, ex_recv, rs_send, rs_recv, own, x_send, x_recv, zsum, z_send, z_recv,
    idx_ref, seed_ref, idxv, inv, idxp, invp,
    sm_sem, ld_sem, wl_sem, ag_ss, ag_rs, wp_ss, wp_rs, id_sem, ex_ss, ex_rs, rs_ss, rs_rs, x_ss, x_rs, z_ss, z_rs, ready,
):
    y = lax.axis_index("dp")
    mp = lax.axis_index("mp")
    core = lax.rem(mp, 2)
    z = lax.rem(lax.div(mp, 2), NZ)
    x = lax.div(mp, 2 * NZ)

    def at(yy, xx, zz, cc):
        return (yy, (xx * NZ + zz) * 2 + cc)

    def wrap(value, size):
        return lax.rem(value + size, size)

    y_dev = (at(wrap(y + 1, NY), x, z, core), at(wrap(y - 1, NY), x, z, core))
    x_dev = (at(y, wrap(x + 1, NX), z, core), at(y, wrap(x - 1, NX), z, core))
    pair_dev = at(y, x, z, 1 - core)

    def z_dev(shift):
        return at(y, x, wrap(z + shift, NZ), core)

    w_hbm = (wi_hbm, wo_hbm)

    barrier = pltpu.get_barrier_semaphore()
    around = (*y_dev, *x_dev, z_dev(1), z_dev(-1), pair_dev)
    for device in around:
        pl.semaphore_signal(barrier, inc=1, device_id=device, device_id_type=MESH)

    small = [
        pltpu.make_async_copy(idx_hbm, idx_ref, sm_sem.at[0]),
        pltpu.make_async_copy(seed_hbm, seed_ref, sm_sem.at[1]),
    ]
    own_w = [
        pltpu.make_async_copy(w_hbm[w].at[0], wg.at[w, pl.ds(2 * y, 2)], wl_sem.at[w])
        for w in range(2)
    ]
    for copy in small + own_w:
        copy.start()
    for j in range(NJ):
        cols = pl.ds(j * BS, BS)
        pltpu.make_async_copy(x_hbm.at[:, cols], x3.at[j], ld_sem.at[0]).start()
        pltpu.make_async_copy(g_hbm.at[:, cols], g3.at[j], ld_sem.at[1]).start()
    pl.semaphore_wait(barrier, len(around))

    def ag_origin(step, way):
        return wrap(y - step if way == 0 else y + step, NY)

    def ag_copy(w, step, way, s):
        hops = 2 if step == NY // 2 else 1
        slot = 2 * ag_origin(step - hops, way) + s
        src = w_hbm[w].at[0, s] if step == 1 else wg.at[w, slot]
        device = at(ag_origin(hops, 1 - way), x, z, core)
        return rdma(src, wg.at[w, slot], ag_ss.at[w], ag_rs.at[w, way, step - 1, s], device)

    def ag_wait(w, step, way, s):
        here = wg.at[w, 2 * ag_origin(step, way) + s]
        rdma(
            here, here, ag_ss.at[w], ag_rs.at[w, way, step - 1, s], y_dev[way]
        ).wait_recv()

    def pass_on(w, slot):
        return rdma(wg.at[w, slot], wp.at[w, slot], wp_ss.at[w], wp_rs.at[w], pair_dev)

    for chain in range(2):
        for w in range(2):
            for way in range(2):
                ag_copy(w, 1, way, way ^ chain).start()
    for w in range(2):
        rdma(
            w_hbm[w].at[0], wp.at[w, pl.ds(2 * y, 2)], wp_ss.at[w], wp_rs.at[w], pair_dev
        ).start()

    for copy in small:
        copy.wait()
    for k in range(K):
        idxv[k] = jnp.where(k < cnt_ref[0], idx_ref[0, k], NJ)
    tables = rdma(idxv, idxp, id_sem.at[0], id_sem.at[1], pair_dev)
    tables.start()

    def invert(src, dst):
        for j in range(NJ):
            found = jnp.int32(K)
            for k in range(K):
                found = jnp.where(src[k] == j, k, found)
            dst[j] = found

    invert(idxv, inv)
    blank = jnp.zeros((BS, BS), BF16)
    x3[NJ] = blank
    g3[NJ] = blank
    wg[0, K] = blank
    wg[1, K] = blank
    wp[0, K] = blank
    wp[1, K] = blank

    rows = lax.broadcasted_iota(jnp.int32, (BS, BS), 0)
    cols = lax.broadcasted_iota(jnp.int32, (BS, BS), 1)
    seeds = jnp.broadcast_to(seed_ref[...], (BS, BS)).T
    mixed = scramble(seeds + (mp * BS + cols) * jnp.int32(668265261))
    keep_ref[...] = jnp.where((mixed & 7) != 0, F32(8.0 / 7.0), F32(0.0))
    half = lax.shift_right_logical(rows, 6)
    tok_x = (x + (lax.shift_right_logical(rows, 4) & 3)) & 3
    tok_z = (z + (rows & 15)) & 15
    tok_c = jnp.where(half == 1, core, 1 - core)
    token = tok_x * 32 + tok_z * 2 + tok_c
    perm_ref[...] = jnp.where(token == cols, F32(1.0), F32(0.0)).astype(BF16)

    for i, ref in enumerate((x3, g3)):
        whole = ref.at[pl.ds(0, NJ)]
        pltpu.make_async_copy(whole, whole, ld_sem.at[i]).wait()

    def ready_round(r):
        for shift in (1 << r, -(1 << r)):
            pl.semaphore_signal(
                ready.at[r], inc=1, device_id=z_dev(shift), device_id_type=MESH
            )

    ready_round(0)

    def two(ref, origin):
        return ref[idxv[2 * origin]], ref[idxv[2 * origin + 1]]

    def pre_part(origin):
        left = jnp.concatenate(two(x3, origin), axis=1)
        right = wg[0, pl.ds(2 * origin, 2)].reshape(2 * BS, BS)
        return mm(left, right)

    def gd_part(origin):
        left = jnp.concatenate(two(g3, origin), axis=1)
        right = jnp.concatenate((wg[1, 2 * origin], wg[1, 2 * origin + 1]), axis=1)
        return mm_t(left, right)

    for copy in own_w:
        copy.wait()

    def ag_step(step, weights=(0, 1)):
        for chain in range(2):
            for w in weights:
                for way in range(2):
                    s = way ^ chain
                    if s in ag_slots(step, way):
                        ag_wait(w, step, way, s)
                        if step + 1 < NY // 2:
                            ag_copy(w, step + 1, way, s).start()
                if chain == 0 and step == NY // 2 - 2:
                    for way in range(2):
                        ag_copy(w, NY // 2, way, way).start()
                for way in range(2):
                    s = way ^ chain
                    if s in ag_slots(step, way):
                        pass_on(w, 2 * ag_origin(step, way) + s).start()

    pre_ref[...] = pre_part(y)
    gd_ref[...] = gd_part(y)
    for step in range(1, NY // 2):
        ag_step(step)
        if step == NY // 2 - 1:
            pl.semaphore_wait(ready.at[0], 2)
            ready_round(1)
        if step == 1:
            for k in range(K):
                x3t[k] = x3[idxv[k]].T
        if step == 2:
            tables.wait()
            invert(idxp, invp)
        left, right = ag_origin(step, 0), ag_origin(step, 1)
        pre_ref[...] += pre_part(left) + pre_part(right)
        gd_ref[...] += gd_part(left) + gd_part(right)

    def swap(t):
        return rdma(ex_send.at[t], ex_recv.at[t], ex_ss, ex_rs.at[t], pair_dev)

    perm = perm_ref[...]
    keep = keep_ref[...]
    far = ag_origin(NY // 2, 0)
    ag_step(NY // 2, (0,))
    activation, slope = gelu_parts(pre_ref[...] + pre_part(far))
    dropped = (activation * keep).astype(BF16)
    slope = slope * keep
    dt_ref[...] = dropped.T
    ordered = mm(perm, dropped).astype(BF16)
    ex_send[0] = ordered[:64]
    mine = [ordered[64:]]
    swap(0).start()

    def term(w, slot):
        if w == 1:
            return mm(dt_ref[...], g3[idxv[slot]])
        return mm(x3t[slot], gp_ref[...])

    def rs_copy(w, step, way, s):
        i = RS_FLAT[step, way, s]
        return rdma(rs_send.at[w, i], rs_recv.at[w, i], rs_ss.at[w], rs_rs.at[w, i], y_dev[way])

    def rs_piece(w, step, way, s):
        far = NY // 2 + 1 - step
        owner = wrap(y + far if way == 0 else y - far, NY)
        value = term(w, 2 * owner + s)
        if step > 1 and s in rs_slots(step - 1, way):
            rs_copy(w, step - 1, way, s).wait_recv()
            value = value + rs_recv[w, RS_FLAT[step - 1, way, s]].astype(F32)
        rs_send[w, RS_FLAT[step, way, s]] = value.astype(BF16)
        rs_copy(w, step, way, s).start()

    def rs_both(w, step, chain):
        for way in range(2):
            rs_piece(w, step, way, way ^ chain)

    def rs_end(w, s):
        value = term(w, 2 * y + s)
        for way in range(2):
            rs_copy(w, NY // 2, way, s).wait_recv()
            value = value + rs_recv[w, RS_FLAT[NY // 2, way, s]].astype(F32)
        (gwi_ref, gwo_ref)[w][0, s] = value

    rs_both(1, 1, 0)
    ag_step(NY // 2, (1,))
    grad_pre = ((gd_ref[...] + gd_part(far)) * slope).astype(BF16)
    gp_ref[...] = grad_pre
    ordered = mm(perm, grad_pre).astype(BF16)
    ex_send[1] = ordered[:64]
    mine.append(ordered[64:])
    swap(1).start()

    def x_copy(g, p):
        sem = x_rs.at[g, min(p, 2)]
        return rdma(x_send.at[g, p], x_recv.at[g, p], x_ss, sem, x_dev[X_WAY[p]])

    def x_own(g, sub, chunk):
        return own[g, pl.ds(sub * HALF, HALF), pl.ds(chunk * 16, 16), :]

    def x_first(g, pieces):
        for p in pieces:
            x_send[g, p] = x_own(g, X_SUB[p], X_CHUNK[p]).astype(BF16)
            x_copy(g, p).start()

    def x_second(g):
        for p in (4, 5):
            x_copy(g, p - 4).wait_recv()
            value = x_own(g, X_SUB[p], X_CHUNK[p]) + x_recv[g, p - 4].astype(F32)
            x_send[g, p] = value.astype(BF16)
            x_copy(g, p).start()

    def z_first(g):
        last = pl.ds(2, 4)
        rdma(x_send.at[g, last], x_recv.at[g, last], x_ss, x_rs.at[g, 2], x_dev[0]).wait_recv()
        for sub, (near, more) in enumerate(((3, 4), (2, 5))):
            value = x_own(g, sub, 0) + x_recv[g, near].astype(F32) + x_recv[g, more].astype(F32)
            zsum[g, pl.ds(sub * HALF * NZ, HALF * NZ)] = value.reshape(HALF * NZ, BS)
        for shift in Z_ORDER:
            z_send[g, shift] = zsum[g, pl.ds(shift, GROUP, stride=NZ), :].astype(BF16)
            rdma(
                z_send.at[g, shift], z_recv.at[g, shift], z_ss, z_rs.at[g], z_dev(shift)
            ).start()

    others = pl.ds(1, NZ - 1)

    def z_end(g):
        rdma(
            z_send.at[g, others], z_recv.at[g, others], z_ss, z_rs.at[g], z_dev(1)
        ).wait_recv()
        total = zsum[g, pl.ds(0, GROUP, stride=NZ), :]
        for shift in Z_ORDER:
            total = total + z_recv[g, shift].astype(F32)
        for i in range(GROUP):
            t, j = divmod(g * GROUP + i, NJ)
            (out_ref, ing_ref)[t][:, j * BS:(j + 1) * BS] = total[i:i + 1].astype(BF16)

    both = []

    def product(u):
        t, j = divmod(u, NJ)

        def pair(j):
            w = 1 - t
            return jnp.concatenate((wg[w, inv[j]], wp[w, invp[j]]), axis=t)

        right = jnp.concatenate((pair(j), pair(j + 1)), axis=1 - t)
        return (mm, mm_t)[t](both[t], right)

    def fill(g):
        for i in range(0, GROUP, 2):
            value = product(g * GROUP + i)
            own[g, i] = value[:, :BS]
            own[g, i + 1] = value[:, BS:]

    for w in range(2):
        here = wp.at[w, pl.ds(0, K)]
        rdma(here, here, wp_ss.at[w], wp_rs.at[w], pair_dev).wait_recv()

    def swap_end(t):
        swap(t).wait_recv()
        both.append(jnp.concatenate((mine[t], ex_recv[t]), axis=1))

    pl.semaphore_wait(ready.at[1], 2)
    ready_round(2)
    rs_both(0, 1, 0)
    swap_end(0)
    fill(0)
    x_first(0, (0, 1))
    fill(1)
    x_first(1, (0, 1))
    swap_end(1)
    for g in range(2, NG):
        fill(g)
        x_first(g, (0, 1))
    rs_both(1, 2, 1)
    rs_both(0, 2, 1)
    for g in range(NG):
        x_first(g, (2, 3))
    rs_both(1, 2, 0)
    x_second(0)
    rs_both(0, 2, 0)
    x_second(1)
    x_second(2)
    rs_both(1, 3, 1)
    x_second(3)
    x_second(4)
    rs_both(0, 3, 1)
    pl.semaphore_wait(ready.at[2], 2)
    z_first(0)
    rs_both(1, 3, 0)
    z_first(1)
    rs_both(0, 3, 0)
    z_first(2)
    rs_both(1, 4, 1)
    z_first(3)
    rs_both(0, 4, 1)
    z_first(4)
    rs_both(1, 4, 0)
    rs_both(0, 4, 0)
    for w in (1, 0):
        rs_end(w, 1)
        rs_end(w, 0)
    for g in range(NG):
        z_end(g)

    for w in range(2):
        here = wg.at[w, pl.ds(0, 14)]
        rdma(here, here, ag_ss.at[w], ag_rs.at[w, 0, 0, 0], y_dev[0]).wait_send()
        rdma(rs_send.at[w], rs_recv.at[w], rs_ss.at[w], rs_rs.at[w, 0], y_dev[0]).wait_send()
        here = wg.at[w, pl.ds(0, K)]
        rdma(here, here, wp_ss.at[w], wp_rs.at[w], pair_dev).wait_send()
    rdma(ex_send, ex_recv, ex_ss, ex_rs.at[0], pair_dev).wait_send()
    rdma(x_send, x_recv, x_ss, x_rs.at[0, 0], x_dev[0]).wait_send()
    rdma(
        z_send.at[:, others], z_recv.at[:, others], z_ss, z_rs.at[0], z_dev(1)
    ).wait_send()


def put_out(*refs):
    copies = [
        pltpu.make_async_copy(refs[i], refs[4 + i], refs[8].at[i]) for i in range(4)
    ]
    for copy in copies:
        copy.start()
    for copy in copies:
        copy.wait()


def body(inputs, cotangent, w_in, w_out, block_index, block_count, drop_seeds):
    vmem = pl.BlockSpec(memory_space=pltpu.VMEM)
    hbm = pl.BlockSpec(memory_space=pltpu.HBM)
    dma = pltpu.SemaphoreType.DMA
    block = (BS, BS)
    results = (
        jax.ShapeDtypeStruct((1, NJ * BS), BF16),
        jax.ShapeDtypeStruct((1, NJ * BS), BF16),
        jax.ShapeDtypeStruct((1, 2, BS, BS), F32),
        jax.ShapeDtypeStruct((1, 2, BS, BS), F32),
    )
    held = pl.pallas_call(
        kernel,
        out_shape=(
            *results,
        ),
        in_specs=[hbm] * 5 + [pl.BlockSpec(memory_space=pltpu.SMEM), hbm],
        out_specs=(vmem,) * 4,
        scratch_shapes=[
            pltpu.VMEM((NJ + 1, *block), BF16),
            pltpu.VMEM((NJ + 1, *block), BF16),
            pltpu.VMEM((K, *block), BF16),
            pltpu.VMEM((2, K + 1, *block), BF16),
            pltpu.VMEM(block, F32),
            pltpu.VMEM(block, BF16),
            pltpu.VMEM(block, F32),
            pltpu.VMEM(block, F32),
            pltpu.VMEM(block, BF16),
            pltpu.VMEM(block, BF16),
            pltpu.VMEM((2, K + 1, *block), BF16),
            pltpu.VMEM((2, 64, BS), BF16),
            pltpu.VMEM((2, 64, BS), BF16),
            pltpu.VMEM((2, 14, *block), BF16),
            pltpu.VMEM((2, 14, *block), BF16),
            pltpu.VMEM((NG, GROUP, 64, BS), F32),
            pltpu.VMEM((NG, 6, HALF, 16, BS), BF16),
            pltpu.VMEM((NG, 6, HALF, 16, BS), BF16),
            pltpu.VMEM((NG, GROUP * NZ, BS), F32),
            pltpu.VMEM((NG, NZ, GROUP, BS), BF16),
            pltpu.VMEM((NG, NZ, GROUP, BS), BF16),
            pltpu.SMEM((1, K), jnp.int32),
            pltpu.VMEM((1, BS), jnp.int32),
            pltpu.SMEM((K,), jnp.int32),
            pltpu.SMEM((NJ,), jnp.int32),
            pltpu.SMEM((K,), jnp.int32),
            pltpu.SMEM((NJ,), jnp.int32),
            dma((2,)),
            dma((2,)),
            dma((2,)),
            dma((2,)),
            dma((2, 2, 4, 2)),
            dma((2,)),
            dma((2,)),
            dma((2,)),
            dma(()),
            dma((2,)),
            dma((2,)),
            dma((2, 14)),
            dma(()),
            dma((NG, 3)),
            dma(()),
            dma((NG,)),
            pltpu.SemaphoreType.REGULAR((3,)),
        ],
        compiler_params=pltpu.CompilerParams(
            collective_id=0, has_side_effects=True, vmem_limit_bytes=40 << 20
        ),
    )(
        *(
            pltpu.with_memory_space_constraint(value, pltpu.HBM)
            for value in (
                inputs, cotangent, w_in, w_out, block_index
            )
        ), block_count, pltpu.with_memory_space_constraint(drop_seeds.reshape(1, BS), pltpu.HBM)
    )
    return pl.pallas_call(
        put_out,
        out_shape=results,
        in_specs=[vmem] * 4,
        out_specs=(hbm,) * 4,
        scratch_shapes=[dma((4,))],
        compiler_params=pltpu.CompilerParams(vmem_limit_bytes=1 << 20),
    )(*held)


def solution(mesh):
    placed = (
        P("dp", None),
        P("dp", None),
        P("mp", "dp", None, None),
        P("mp", "dp", None, None),
        P("mp", None),
        P("mp"),
        P("dp"),
    )
    return jax.shard_map(
        body,
        mesh=mesh,
        in_specs=placed,
        out_specs=(
            P(("dp", "mp"), None),
            P(("dp", "mp"), None),
            P("mp", "dp", None, None),
            P("mp", "dp", None, None),
        ),
        check_vma=False,
    )
```
